32 devices in a mesh: ctx: 8 (over z, y), fsdp: 4 (over x, core).
Axes of the slice: x: 2, y: 2, z: 4, core: 2. Of those that a mesh axis runs over, the one named last changes fastest.
Arguments:
- tokens: bfloat16 [4, 1024, 1600], P('fsdp', 'ctx'), may hold values from -6 to 6
- cotangent: bfloat16 [4, 1024, 1600], P('fsdp', 'ctx'), may hold values from -6 to 6
- segment_ids: int32 [4, 1024], P('fsdp'), may hold values from 0 to 3, never falling along the last dimension, each value on 1 to 768 neighbouring positions
- attn_norm_gain: float32 [1600], replicated, may hold values from 0.5 to 1.5
- w_query: bfloat16 [1600, 1600], P('ctx', 'fsdp'), may hold values from -0.18 to 0.18
- w_keyval: bfloat16 [1600, 640], P('ctx', 'fsdp'), may hold values from -0.15625 to 0.15625
- meta_keyvals: bfloat16 [128, 640], replicated, may hold values from -6 to 6
- w_attn_out: bfloat16 [1600, 1600], P('ctx', 'fsdp'), may hold values from -0.15625 to 0.15625
- w_mamba_in: bfloat16 [1600, 6400], P('ctx', 'fsdp'), may hold values from -0.15625 to 0.15625
- w_control: bfloat16 [1600, 82], replicated, may hold values from -0.15625 to 0.15625
- conv_weight: float32 [4, 3200], replicated, may hold values from -3 to 3
- conv_bias: float32 [3200], replicated, may hold values from -0.5 to 0.5
- step_bias: float32 [50], replicated, may hold values from -6 to -3
- decay_log: float32 [50], replicated, may hold values from -5 to 1
- skip_gain: float32 [3200], replicated, may hold values from 0.5 to 1.5
- w_ssm_out: bfloat16 [3200, 1600], P('ctx', 'fsdp'), may hold values from -0.109375 to 0.109375
- beta_attn: float32 [1600], replicated, may hold values from 0.5 to 1.5
- beta_ssm: float32 [1600], replicated, may hold values from 0.5 to 1.5
- mlp_norm_gain: float32 [1600], replicated, may hold values from 0.5 to 1.5
- w_gate_up: bfloat16 [1600, 11008], P('ctx', 'fsdp'), may hold values from -0.15625 to 0.15625
- w_down: bfloat16 [5504, 1600], P('ctx', 'fsdp'), may hold values from -0.078125 to 0.078125
Outputs:
- output: bfloat16 [4, 1024, 1600], P('fsdp', 'ctx')
- grad_tokens: float32 [4, 1024, 1600], P('fsdp', 'ctx')
- grad_attn_norm_gain: float32 [1600], replicated
- grad_w_query: float32 [1600, 1600], P('ctx', 'fsdp')
- grad_w_keyval: float32 [1600, 640], P('ctx', 'fsdp')
- grad_meta_keyvals: float32 [128, 640], replicated
- grad_w_attn_out: float32 [1600, 1600], P('ctx', 'fsdp')
- grad_w_mamba_in: float32 [1600, 6400], P('ctx', 'fsdp')
- grad_w_control: float32 [1600, 82], replicated
- grad_conv_weight: float32 [4, 3200], replicated
- grad_conv_bias: float32 [3200], replicated
- grad_step_bias: float32 [50], replicated
- grad_decay_log: float32 [50], replicated
- grad_skip_gain: float32 [3200], replicated
- grad_w_ssm_out: float32 [3200, 1600], P('ctx', 'fsdp')
- grad_beta_attn: float32 [1600], replicated
- grad_beta_ssm: float32 [1600], replicated
- grad_mlp_norm_gain: float32 [1600], replicated
- grad_w_gate_up: float32 [1600, 11008], P('ctx', 'fsdp')
- grad_w_down: float32 [5504, 1600], P('ctx', 'fsdp')
The draws below stay inside these ranges and needn't reach their ends.
Inputs may be any that keep to these rules, and one draw needn't show every extreme that they name: `segment_ids`: within a row the numbers never fall; each segment spans 1 to 768 positions and one spans exactly 768.
All inputs are finite; a program needn't handle non-finite values.
Results may differ from the reference program's by a relative error of at most 0.03.
Values may be sent and summed in bfloat16 or wider, within the bound.
No kernel may reach another device: no remote copies, remote signals or barrier semaphores. Data moves between devices by JAX's collectives and lax.ppermute only.
A program may use at most 256 MiB of HBM per device.

```python
import math
import jax
import jax.numpy as jnp
import numpy as np
from jax import lax

D = 1600
HEADS = 25
KV_HEADS = 5
HEAD_DIM = 64
META = 128
INNER = 3200
STATE = 16
CONV = 4
SSM_HEAD = 64
FF = 5504
TOK_DEV = 128
DOCS = 4
QD = 1600
KVD = 320
SSM_HEADS = 50
SEQ = 1024
SEQS = 4
DOC_MOST = 768


def draw_tokens(key, part):
    noise = jnp.clip(jax.random.normal(jax.random.fold_in(key, 1), (SEQS, SEQ, D), jnp.float32), -6.0, 6.0)
    return noise.astype(jnp.bfloat16)


def draw_w_query(key, part):
    scale = D ** (-0.5)
    base = jnp.clip(jax.random.normal(jax.random.fold_in(key, 11), (D, QD), jnp.float32), -6.0, 6.0) * scale
    return base.astype(jnp.bfloat16)


def draw_meta_keyvals(key, part):
    base = jnp.clip(jax.random.normal(jax.random.fold_in(key, 21), (META, 2 * KVD), jnp.float32), -6.0, 6.0)
    return base.astype(jnp.bfloat16)


def block_levels(rng, dims, cuts, low, high):
    def one(axis_at, parts):
        draws = jax.random.uniform(jax.random.fold_in(jax.random.fold_in(rng, 6), axis_at), (parts,), jnp.float32, low / len(cuts), high / len(cuts))
        return jnp.repeat(jnp.exp(draws), dims[axis_at] // parts).reshape((-1,) + (1,) * (len(dims) - axis_at - 1))

    level = one(*cuts[0])
    for cut in cuts[1:]:
        level = level * one(*cut)
    return level


def length_profile(count, total, bound, skew):
    portions = [(1 << 20) // math.isqrt(rank ** skew) + 1 for rank in range(2, count + 1)]
    surplus, holding = total - bound - (count - 1), [1] * (count - 1)
    while surplus > 0:
        free = [i for i in range(count - 1) if holding[i] < bound]
        pool, budget = sum([portions[i] for i in free]), surplus
        for i in free:
            extra = min(bound - holding[i], max(1, budget * portions[i] // pool), surplus)
            holding[i] = holding[i] + extra
            surplus = surplus - extra
    return np.array([bound] + holding)


def uneven(stream_key, amount, total, reach, slope):
    if amount == 2:
        one = jax.random.randint(stream_key, (), max(1, total - reach), min(reach, total - 1) + 1)
        return jnp.stack([one, total - one])
    lengths = jnp.asarray(length_profile(amount, total, reach, slope), jnp.int32)
    pairs = (amount - 1) // 2
    donor, taker = lengths[1:1 + 2 * pairs:2], lengths[2:2 + 2 * pairs:2]
    room = jnp.minimum(donor - 1, reach - taker)
    shifted = jax.random.randint(jax.random.fold_in(stream_key, 1), (pairs,), 0, 1 << 20) % (room + 1)
    lengths = lengths.at[1:1 + 2 * pairs:2].set(donor - shifted).at[2:2 + 2 * pairs:2].set(taker + shifted)
    return lengths[jax.random.permutation(jax.random.fold_in(stream_key, 2), amount)]


def gaussian(key, shape, deviation, limit, split=(), kind=jnp.bfloat16):
    factor_of = block_levels(key, shape, split, -0.22, 0.18) if split else 1.0
    array = jax.random.normal(key, shape, jnp.float32) * deviation * factor_of
    return jnp.minimum(jnp.maximum(array, -limit), limit).astype(kind)


def setup_inputs(seed: int = 0) -> dict:
    seeds = jax.random.split(jax.random.key(seed), 22)
    tokens = draw_tokens(jax.random.fold_in(seeds[21], 71), 0)
    cotangent = gaussian(seeds[1], (SEQS, SEQ, D), 1.0, 6.0, ((0, 4), (1, 8)))
    segment_ids = jax.vmap(lambda own: jnp.searchsorted(jnp.cumsum(uneven(own, DOCS, SEQ, DOC_MOST, 0)), jnp.arange(SEQ), side="right"))(jax.random.split(seeds[2], SEQS)).reshape((SEQS, SEQ)).astype(jnp.int32)
    attn_norm_gain = jnp.clip(1.0 + 0.1 * jax.random.normal(seeds[3], (D,), jnp.float32), 0.5, 1.5)
    w_query = draw_w_query(jax.random.fold_in(seeds[21], 71), 0)
    w_keyval = gaussian(seeds[5], (D, 2 * KVD), D ** -0.5, 0.15625, ((0, 8), (1, 4)))
    meta_keyvals = draw_meta_keyvals(jax.random.fold_in(seeds[21], 71), 0)
    w_attn_out = gaussian(seeds[7], (QD, D), QD ** -0.5, 0.15625, ((0, 8), (1, 4)))
    w_mamba_in = gaussian(seeds[8], (D, 2 * INNER), D ** -0.5, 0.15625, ((0, 8), (1, 4)))
    w_control = gaussian(seeds[9], (D, 2 * STATE + SSM_HEADS), D ** -0.5, 0.15625)
    conv_weight = gaussian(seeds[10], (CONV, INNER), 0.5, 3.0, (), jnp.float32)
    conv_bias = jnp.clip(jax.random.uniform(seeds[11], (INNER,), jnp.float32, -0.5, 0.5), -0.5, 0.5)
    step_bias = jnp.clip(jax.random.uniform(seeds[12], (SSM_HEADS,), jnp.float32, -6.0, -3.0), -6.0, -3.0)
    decay_log = jnp.clip(jax.random.uniform(seeds[13], (SSM_HEADS,), jnp.float32, -5.0, 1.0), -5.0, 1.0)
    skip_gain = jnp.clip(jax.random.uniform(seeds[14], (INNER,), jnp.float32, 0.5, 1.5), 0.5, 1.5)
    w_ssm_out = gaussian(seeds[15], (INNER, D), INNER ** -0.5, 0.109375, ((0, 8), (1, 4)))
    beta_attn = jnp.clip(1.0 + 0.1 * jax.random.normal(seeds[16], (D,), jnp.float32), 0.5, 1.5)
    beta_ssm = jnp.clip(1.0 + 0.1 * jax.random.normal(seeds[17], (D,), jnp.float32), 0.5, 1.5)
    mlp_norm_gain = jnp.clip(1.0 + 0.1 * jax.random.normal(seeds[18], (D,), jnp.float32), 0.5, 1.5)
    w_gate_up = gaussian(seeds[19], (D, 2 * FF), D ** -0.5, 0.15625, ((0, 8), (1, 4)))
    w_down = gaussian(seeds[20], (FF, D), FF ** -0.5, 0.078125, ((0, 8), (1, 4)))
    return {"tokens": tokens, "cotangent": cotangent, "segment_ids": segment_ids, "attn_norm_gain": attn_norm_gain, "w_query": w_query, "w_keyval": w_keyval, "meta_keyvals": meta_keyvals, "w_attn_out": w_attn_out, "w_mamba_in": w_mamba_in, "w_control": w_control, "conv_weight": conv_weight, "conv_bias": conv_bias, "step_bias": step_bias, "decay_log": decay_log, "skip_gain": skip_gain, "w_ssm_out": w_ssm_out, "beta_attn": beta_attn, "beta_ssm": beta_ssm, "mlp_norm_gain": mlp_norm_gain, "w_gate_up": w_gate_up, "w_down": w_down}


epsilon = 1e-05
masked_score = -1e+30
highest = lax.Precision.HIGHEST

def rms_norm(values, gain):
    return values * lax.rsqrt(lax.optimization_barrier(jnp.mean(values * values, axis=-1, keepdims=True)) + epsilon) * gain

def branch_mix(attn_part, ssm_part, beta_attn, beta_ssm):
    return 0.5 * (rms_norm(attn_part, beta_attn) + rms_norm(ssm_part, beta_ssm))

def gated_unit(gate_up):
    half = gate_up.shape[-1] // 2
    return jax.nn.silu(gate_up[:, :half]) * gate_up[:, half:]

def rounded(values):
    return lax.optimization_barrier(values.astype(jnp.bfloat16)).astype(jnp.float32)

def mamba_prepare(mamba_rows, control, previous, seg_window, conv_weight, conv_bias, step_bias, decay_log):
    kernel = conv_weight.shape[0]
    width = conv_weight.shape[1]
    length = mamba_rows.shape[0]
    x_part = mamba_rows[:, :width]
    z_part = mamba_rows[:, width:]
    extended = jnp.concatenate([previous, x_part], axis=0)
    seg_rows = seg_window[kernel - 1:]
    convolved = conv_bias + jnp.zeros_like(x_part)
    for offset in range(kernel):
        same_doc = (seg_window[offset:offset + length] == seg_rows).astype(jnp.float32)
        convolved = convolved + conv_weight[offset] * extended[offset:offset + length] * same_doc[:, None]
    activated = jax.nn.silu(convolved)
    head_count = decay_log.shape[0]
    state_size = (control.shape[1] - head_count) // 2
    write_map = control[:, :state_size]
    read_map = control[:, state_size:2 * state_size]
    step_size = jax.nn.softplus(control[:, 2 * state_size:] + step_bias)
    log_decay = jnp.cumsum(-jnp.exp(decay_log) * step_size, axis=0)
    return (activated, z_part, write_map, read_map, step_size, log_decay, seg_rows)

def mamba_state(prepared, seg_before):
    activated, z_part, write_map, read_map, step_size, log_decay, seg_rows = prepared
    length = activated.shape[0]
    head_count = step_size.shape[1]
    scaled = activated.reshape(length, head_count, SSM_HEAD) * step_size[:, :, None]
    same_end = (seg_rows == seg_rows[length - 1]).astype(jnp.float32)
    to_end = jnp.exp(log_decay[length - 1][None, :] - log_decay) * same_end[:, None]
    state_sum = jnp.einsum('th,thp,tn->hpn', to_end, scaled, write_map, precision=highest)
    through = jnp.exp(log_decay[length - 1]) * (seg_rows[length - 1] == seg_before).astype(jnp.float32)
    return (through, state_sum)

def mamba_output(prepared, seg_before, state_in, skip_gain):
    activated, z_part, write_map, read_map, step_size, log_decay, seg_rows = prepared
    length = activated.shape[0]
    head_count = step_size.shape[1]
    scaled = activated.reshape(length, head_count, SSM_HEAD) * step_size[:, :, None]
    positions = jnp.arange(length)
    allowed = ((positions[:, None] >= positions[None, :]) & (seg_rows[:, None] == seg_rows[None, :])).astype(jnp.float32)
    decay_heads = log_decay.T
    gaps = decay_heads[:, :, None] - decay_heads[:, None, :]
    within = jnp.exp(jnp.minimum(gaps, 0.0)) * allowed[None]
    intersection = jnp.einsum('tn,rn->tr', read_map, write_map, precision=highest)
    results = jnp.einsum('htr,rhp->thp', within * intersection[None], scaled, precision=highest)
    carried = jnp.exp(log_decay) * (seg_rows == seg_before).astype(jnp.float32)[:, None]
    results = results + jnp.einsum('th,tn,hpn->thp', carried, read_map, state_in, precision=highest)
    results = results.reshape(length, -1) + skip_gain * activated
    return results * jax.nn.silu(z_part)

def mamba_sequence(mamba_all, control_all, seg, conv_weight, conv_bias, step_bias, decay_log, skip_gain):
    kernel = conv_weight.shape[0]
    width = conv_weight.shape[1]
    length = TOK_DEV
    blocks = mamba_all.shape[0] // length
    head_count = decay_log.shape[0]
    state_size = (control_all.shape[1] - head_count) // 2
    padded_x = jnp.concatenate([jnp.zeros((kernel - 1, width), jnp.float32), mamba_all[:, :width]], axis=0)
    padded_seg = jnp.concatenate([jnp.full((kernel - 1,), -1, jnp.int32), seg.astype(jnp.int32)])

    def advance(state_in, block_id):
        anchor = (block_id * length).astype(jnp.int32)
        rows_here = lax.dynamic_slice_in_dim(mamba_all, anchor, length, 0)
        control_here = lax.dynamic_slice_in_dim(control_all, anchor, length, 0)
        previous = lax.dynamic_slice_in_dim(padded_x, anchor, kernel - 1, 0)
        seg_window = lax.dynamic_slice_in_dim(padded_seg, anchor, length + kernel - 1, 0)
        seg_before = seg_window[kernel - 2]
        prepared = mamba_prepare(rows_here, control_here, previous, seg_window, conv_weight, conv_bias, step_bias, decay_log)
        through, state_sum = mamba_state(prepared, seg_before)
        results = mamba_output(prepared, seg_before, state_in, skip_gain)
        return (through[:, None, None] * state_in + state_sum, results)
    state_zero = jnp.zeros((head_count, width // head_count, state_size), jnp.float32)
    final_state, results = lax.scan(advance, state_zero, jnp.arange(blocks, dtype=jnp.int32))
    return results.reshape(blocks * length, width)

def split_keys(meta_keyvals, keyvals):
    kv_width = KV_HEADS * HEAD_DIM
    keys_all = jnp.concatenate([meta_keyvals[:, :kv_width], keyvals[:, :kv_width]], axis=0)
    values_all = jnp.concatenate([meta_keyvals[:, kv_width:], keyvals[:, kv_width:]], axis=0)
    keys_all = keys_all.astype(jnp.float32).reshape(-1, KV_HEADS, HEAD_DIM)
    values_all = values_all.astype(jnp.float32).reshape(-1, KV_HEADS, HEAD_DIM)
    return (keys_all, values_all)

def visibility(seg, anchor):
    seq_len = seg.shape[0]
    key_pos = jnp.arange(seq_len, dtype=jnp.int32)
    query_pos = anchor + jnp.arange(TOK_DEV, dtype=jnp.int32)
    query_seg = lax.dynamic_slice_in_dim(seg, anchor, TOK_DEV, 0)
    local = (key_pos[None, :] <= query_pos[:, None]) & (seg[None, :] == query_seg[:, None])
    return jnp.concatenate([jnp.full((TOK_DEV, META), True), local], axis=1)

def attention_forward(queries, keyvals, meta_keyvals, seg):
    seq_len = queries.shape[0]
    group = HEADS // KV_HEADS
    scale_q = HEAD_DIM ** (-0.5)
    keys_all, values_all = split_keys(meta_keyvals, keyvals)
    blocks = seq_len // TOK_DEV

    def one_block(block_id):
        anchor = (block_id * TOK_DEV).astype(jnp.int32)
        query_rows = lax.dynamic_slice_in_dim(queries, anchor, TOK_DEV, 0).astype(jnp.float32)
        query_rows = query_rows.reshape(TOK_DEV, KV_HEADS, group, HEAD_DIM)
        visible = visibility(seg, anchor)
        scores = jnp.einsum('tkgd,skd->kgts', query_rows, keys_all) * scale_q
        scores = jnp.where(visible[None, None], scores, masked_score)
        peak = lax.optimization_barrier(jnp.max(scores, axis=-1))
        expo = jnp.exp(scores - peak[..., None])
        totals = lax.optimization_barrier(jnp.sum(expo, axis=-1))
        context = jnp.einsum('kgts,skd->tkgd', rounded(expo), values_all)
        context = context / jnp.transpose(totals, (2, 0, 1))[..., None]
        return (context.reshape(TOK_DEV, HEADS * HEAD_DIM).astype(jnp.bfloat16), peak + jnp.log(totals))
    contexts, log_sums = lax.map(one_block, jnp.arange(blocks, dtype=jnp.int32))
    return (contexts.reshape(seq_len, HEADS * HEAD_DIM), log_sums)

def attention_backward(queries, keyvals, meta_keyvals, seg, contexts, log_sums, grad_context):
    seq_len = queries.shape[0]
    group = HEADS // KV_HEADS
    scale_q = HEAD_DIM ** (-0.5)
    kv_width = KV_HEADS * HEAD_DIM
    keys_all, values_all = split_keys(meta_keyvals, keyvals)
    blocks = seq_len // TOK_DEV

    def one_block(running, block_id):
        grad_keys, grad_values = running
        anchor = (block_id * TOK_DEV).astype(jnp.int32)
        shape_rows = (TOK_DEV, KV_HEADS, group, HEAD_DIM)
        query_rows = lax.dynamic_slice_in_dim(queries, anchor, TOK_DEV, 0).astype(jnp.float32).reshape(shape_rows)
        grad_rows = lax.dynamic_slice_in_dim(grad_context, anchor, TOK_DEV, 0).astype(jnp.float32).reshape(shape_rows)
        context_rows = lax.dynamic_slice_in_dim(contexts, anchor, TOK_DEV, 0).astype(jnp.float32).reshape(shape_rows)
        deltas = jnp.einsum('tkgd,tkgd->kgt', grad_rows, context_rows)
        visible = visibility(seg, anchor)
        scores = jnp.einsum('tkgd,skd->kgts', query_rows, keys_all) * scale_q
        scores = jnp.where(visible[None, None], scores, masked_score)
        probs = jnp.exp(scores - log_sums[block_id][..., None])
        grad_values = grad_values + jnp.einsum('kgts,tkgd->skd', rounded(probs), grad_rows)
        grad_probs = jnp.einsum('tkgd,skd->kgts', grad_rows, values_all)
        grad_scores = rounded(probs * (grad_probs - deltas[..., None]))
        grad_query = jnp.einsum('kgts,skd->tkgd', grad_scores, keys_all) * scale_q
        grad_keys = grad_keys + jnp.einsum('kgts,tkgd->skd', grad_scores, query_rows) * scale_q
        return ((grad_keys, grad_values), grad_query.reshape(TOK_DEV, HEADS * HEAD_DIM))
    zero_keys = jnp.zeros((META + seq_len, KV_HEADS, HEAD_DIM), jnp.float32)
    (grad_keys, grad_values), grad_queries = lax.scan(one_block, (zero_keys, zero_keys), jnp.arange(blocks, dtype=jnp.int32))
    grad_kv = jnp.concatenate([grad_keys.reshape(-1, kv_width), grad_values.reshape(-1, kv_width)], axis=1)
    return (grad_queries.reshape(seq_len, HEADS * HEAD_DIM), grad_kv[META:], grad_kv[:META])

def matmul(left, right):
    return jnp.dot(left, right, preferred_element_type=jnp.float32)

def one_sequence(params, tokens_row, cotangent_row, seg):
    attn_norm_gain, w_query, w_keyval, meta_keyvals, w_attn_out, w_mamba_in, w_control, conv_weight, conv_bias, step_bias, decay_log, skip_gain, w_ssm_out, beta_attn, beta_ssm, mlp_norm_gain, w_gate_up, w_down = params
    inputs = tokens_row.astype(jnp.float32)
    normed_f32, norm1_pullback = jax.vjp(rms_norm, inputs, attn_norm_gain)
    normed = normed_f32.astype(jnp.bfloat16)
    queries = matmul(normed, w_query).astype(jnp.bfloat16)
    keyvals = matmul(normed, w_keyval).astype(jnp.bfloat16)
    mamba_rows = matmul(normed, w_mamba_in)
    control = matmul(normed, w_control)
    contexts, log_sums = attention_forward(queries, keyvals, meta_keyvals, seg)

    def ssm_branch(rows_in, control_in, cw_in, cb_in, sb_in, dl_in, sk_in):
        return mamba_sequence(rows_in, control_in, seg, cw_in, cb_in, sb_in, dl_in, sk_in)
    ssm_f32, ssm_pullback = jax.vjp(ssm_branch, mamba_rows, control, conv_weight, conv_bias, step_bias, decay_log, skip_gain)
    ssm_rows = ssm_f32.astype(jnp.bfloat16)
    attn_part = matmul(contexts, w_attn_out)
    ssm_part = matmul(ssm_rows, w_ssm_out)
    mixed, mix_pullback = jax.vjp(branch_mix, attn_part, ssm_part, beta_attn, beta_ssm)
    hidden = inputs + mixed
    normed2_f32, norm2_pullback = jax.vjp(rms_norm, hidden, mlp_norm_gain)
    normed2 = normed2_f32.astype(jnp.bfloat16)
    gate_up = matmul(normed2, w_gate_up)
    activation_f32, gate_pullback = jax.vjp(gated_unit, gate_up)
    activation = activation_f32.astype(jnp.bfloat16)
    output = (hidden + matmul(activation, w_down)).astype(jnp.bfloat16)
    grad_w_down = matmul(activation.T, cotangent_row)
    grad_act = matmul(cotangent_row, w_down.T)
    grad_gate_up = gate_pullback(grad_act)[0].astype(jnp.bfloat16)
    grad_w_gate_up = matmul(normed2.T, grad_gate_up)
    grad_normed2 = matmul(grad_gate_up, w_gate_up.T)
    grad_hidden_part, grad_mlp_norm_gain = norm2_pullback(grad_normed2)
    grad_hidden = cotangent_row.astype(jnp.float32) + grad_hidden_part
    grad_attn_f, grad_ssm_f, grad_beta_attn, grad_beta_ssm = mix_pullback(grad_hidden)
    grad_attn = grad_attn_f.astype(jnp.bfloat16)
    grad_ssm = grad_ssm_f.astype(jnp.bfloat16)
    grad_w_attn_out = matmul(contexts.T, grad_attn)
    grad_context = matmul(grad_attn, w_attn_out.T).astype(jnp.bfloat16)
    grad_w_ssm_out = matmul(ssm_rows.T, grad_ssm)
    grad_ssm_rows = matmul(grad_ssm, w_ssm_out.T)
    grad_mamba_f, grad_control_f, grad_conv_weight, grad_conv_bias, grad_step_bias, grad_decay_log, grad_skip_gain = ssm_pullback(grad_ssm_rows)
    grad_mamba_rows = grad_mamba_f.astype(jnp.bfloat16)
    grad_control = grad_control_f.astype(jnp.bfloat16)
    grad_query_f, grad_kv_f, grad_meta_keyvals = attention_backward(queries, keyvals, meta_keyvals, seg, contexts, log_sums, grad_context)
    grad_queries = grad_query_f.astype(jnp.bfloat16)
    grad_keyvals = grad_kv_f.astype(jnp.bfloat16)
    grad_w_query = matmul(normed.T, grad_queries)
    grad_w_keyval = matmul(normed.T, grad_keyvals)
    grad_w_mamba_in = matmul(normed.T, grad_mamba_rows)
    grad_w_control = matmul(normed.T, grad_control)
    grad_normed = matmul(grad_queries, w_query.T) + matmul(grad_keyvals, w_keyval.T) + matmul(grad_mamba_rows, w_mamba_in.T) + matmul(grad_control, w_control.T)
    grad_in_part, grad_attn_norm_gain = norm1_pullback(grad_normed)
    grad_tokens = grad_hidden + grad_in_part
    grads = (grad_attn_norm_gain, grad_w_query, grad_w_keyval, grad_meta_keyvals, grad_w_attn_out, grad_w_mamba_in, grad_w_control, grad_conv_weight, grad_conv_bias, grad_step_bias, grad_decay_log, grad_skip_gain, grad_w_ssm_out, grad_beta_attn, grad_beta_ssm, grad_mlp_norm_gain, grad_w_gate_up, grad_w_down)
    return (output, grad_tokens, grads)

def reference(tokens, cotangent, segment_ids, attn_norm_gain, w_query, w_keyval, meta_keyvals, w_attn_out, w_mamba_in, w_control, conv_weight, conv_bias, step_bias, decay_log, skip_gain, w_ssm_out, beta_attn, beta_ssm, mlp_norm_gain, w_gate_up, w_down):
    params = (attn_norm_gain, w_query, w_keyval, meta_keyvals, w_attn_out, w_mamba_in, w_control, conv_weight, conv_bias, step_bias, decay_log, skip_gain, w_ssm_out, beta_attn, beta_ssm, mlp_norm_gain, w_gate_up, w_down)

    def per_sequence(running, item):
        tokens_row, cotangent_row, seg = item
        output, grad_tokens, grads = one_sequence(params, tokens_row, cotangent_row, seg)
        return (tuple((total + grad for total, grad in zip(running, grads))), (output, grad_tokens))
    zeros = tuple((jnp.zeros(param.shape, jnp.float32) for param in params))
    totals, (outputs, grad_tokens) = lax.scan(per_sequence, zeros, (tokens, cotangent, segment_ids))
    return (outputs, grad_tokens, totals[0], totals[1], totals[2], totals[3], totals[4], totals[5], totals[6], totals[7], totals[8], totals[9], totals[10], totals[11], totals[12], totals[13], totals[14], totals[15], totals[16], totals[17])
```

```python
import math

import jax
import jax.numpy as jnp
from jax import lax
from jax.experimental import pallas as pl
from jax.experimental.pallas import tpu as pltpu
from jax.sharding import PartitionSpec as P

HEADS = 25
KV_HEADS = 5
HEAD_DIM = 64
SSM_HEAD = 64
SLOTS = 13

epsilon = 1e-05
masked_score = -1e30
highest = lax.Precision.HIGHEST
bf16 = jnp.bfloat16
f32 = jnp.float32


def swap(value, axis, mask):
    count = lax.axis_size(axis)
    return lax.ppermute(value, axis, [(source, source ^ mask) for source in range(count)])


def shift_z(value, steps):
    count = lax.axis_size("ctx")
    return lax.ppermute(value, "ctx", [(s, (s + 2 * steps) % count) for s in range(count)])


def passed_along(value, axis, steps):
    count = lax.axis_size(axis)
    first, last = (max(0, -steps), min(count, count - steps))
    return lax.ppermute(value, axis, [(source, source + steps) for source in range(first, last)])


def gather_rows(value):
    far = swap(value, "fsdp", 2)
    near = swap(value, "fsdp", 1)
    return jnp.stack([value, near, far, swap(far, "fsdp", 1)])


def sum_rows(parts):
    received = swap(jnp.stack([parts[1], parts[3]]).astype(bf16), "fsdp", 1).astype(f32)
    mine = parts[0] + received[0]
    far = parts[2] + received[1]
    return mine + swap(far.astype(bf16), "fsdp", 2).astype(f32)


def exchange(parts):
    return [parts[0]] + [swap(parts[k], "fsdp", k) for k in (1, 2, 3)]


def by_member(parts):
    place = lax.axis_index("fsdp")

    def pick(b):
        near = jnp.where(place == 0, parts[b], parts[b ^ 1])
        return jnp.where(place < 2, near, jnp.where(place == 2, parts[b ^ 2], parts[b ^ 3]))

    return [pick(b) for b in range(4)]


def z_groups():
    count = lax.axis_size("ctx")
    return [[2 * z + y for z in range(count // 2)] for y in range(2)]


def odd():
    return lax.axis_index("ctx") % 2 == 1


def own_first(even_part, odd_part):
    return (jnp.where(odd(), odd_part, even_part), jnp.where(odd(), even_part, odd_part))


def halves(values, axis):
    count = lax.axis_size("ctx")
    shape = values.shape
    length = shape[axis] // count
    view = values.reshape(shape[:axis] + (count // 2, 2, length) + shape[axis + 1 :])
    merged = shape[:axis] + (shape[axis] // 2,) + shape[axis + 1 :]
    even = lax.index_in_dim(view, 0, axis + 1, False).reshape(merged)
    odd_part = lax.index_in_dim(view, 1, axis + 1, False).reshape(merged)
    return (even, odd_part)


def joined(even, odd_part, axis):
    count = lax.axis_size("ctx")
    shape = even.shape
    split = shape[:axis] + (count // 2, shape[axis] // (count // 2)) + shape[axis + 1 :]
    both = jnp.stack([even.reshape(split), odd_part.reshape(split)], axis=axis + 1)
    return both.reshape(shape[:axis] + (2 * shape[axis],) + shape[axis + 1 :])


def gather_weight(shard):
    own = lax.all_gather(shard, "ctx", axis=0, tiled=True, axis_index_groups=z_groups())
    return (own, swap(own, "ctx", 1))


def reduce_weight(keep, send):
    total = keep + swap(send.astype(bf16), "ctx", 1).astype(f32)
    count = lax.axis_size("ctx") // 2
    blocks = total.astype(bf16).reshape(count, total.shape[0] // count, total.shape[1])
    return lax.psum_scatter(
        blocks, "ctx", scatter_dimension=0, tiled=False, axis_index_groups=z_groups()
    )


def all_sum(flat):
    steps = []
    for axis in ("fsdp", "ctx"):
        mask = 1
        while mask < lax.axis_size(axis):
            steps.append((axis, mask))
            mask *= 2
    for axis, mask in steps:
        half = flat.shape[0] // 2
        high = (lax.axis_index(axis) // mask) % 2 == 1
        low_part, high_part = flat[:half], flat[half:]
        received = swap(jnp.where(high, low_part, high_part), axis, mask)
        flat = jnp.where(high, high_part, low_part) + received
    for axis, mask in reversed(steps):
        high = (lax.axis_index(axis) // mask) % 2 == 1
        received = swap(flat, axis, mask)
        flat = jnp.concatenate(
            [jnp.where(high, received, flat), jnp.where(high, flat, received)], axis=0
        )
    return flat


def all_sum_small(value):
    for axis in ("fsdp", "ctx"):
        mask = 1
        while mask < lax.axis_size(axis):
            value = value + swap(value, axis, mask)
            mask *= 2
    return value


def rms_norm(values, gain):
    return values * lax.rsqrt(jnp.mean(values * values, axis=-1, keepdims=True) + epsilon) * gain


def branch_mix(attn_part, ssm_part, beta_attn, beta_ssm):
    return 0.5 * (rms_norm(attn_part, beta_attn) + rms_norm(ssm_part, beta_ssm))


def dot(left, right):
    return lax.dot_general(
        left, right, (((left.ndim - 1,), (0,)), ((), ())), preferred_element_type=f32
    )


def dot_t(left, right):
    return lax.dot_general(
        left, right, (((left.ndim - 1,), (1,)), ((), ())), preferred_element_type=f32
    )


def dot_rows(left, right):
    dims = tuple(range(left.ndim - 1))
    return lax.dot_general(left, right, ((dims, dims), ((), ())), preferred_element_type=f32)


def nn(left, right):
    return lax.dot_general(left, right, (((1,), (0,)), ((), ())), preferred_element_type=f32)


def nt(left, right):
    return lax.dot_general(left, right, (((1,), (1,)), ((), ())), preferred_element_type=f32)


def tn(left, right):
    return lax.dot_general(left, right, (((0,), (0,)), ((), ())), preferred_element_type=f32)


def exact(left, right):
    return lax.dot_general(
        left, right, (((1,), (0,)), ((), ())), precision=highest, preferred_element_type=f32
    )


PAD_HEADS = 16


def spread_matrix(width):
    head = lax.broadcasted_iota(jnp.int32, (PAD_HEADS, width), 0)
    column = lax.broadcasted_iota(jnp.int32, (PAD_HEADS, width), 1)
    return jnp.where(column // SSM_HEAD == head, 1.0, 0.0).astype(bf16)


def shifted_down(values, before, steps):
    moved = pltpu.roll(values, steps, 0)
    row = lax.broadcasted_iota(jnp.int32, before.shape, 0)
    top = jnp.where(row < steps, pltpu.roll(before, steps, 0), moved[:8])
    return jnp.concatenate([top, moved[8:]], axis=0)


def conv_input(x, before, masks, cw_ref, cb_ref):
    total = cb_ref[...] + cw_ref[3:4, :] * x
    for steps in (1, 2, 3):
        mask = masks[:, 3 - steps : 4 - steps]
        total = total + cw_ref[3 - steps : 4 - steps, :] * (shifted_down(x, before, steps) * mask)
    return total


def head_steps(raw, sb_ref, dl_ref):
    length = raw.shape[0]
    step = jax.nn.softplus(raw + sb_ref[...])
    rate = -jnp.exp(dl_ref[...])
    row = lax.broadcasted_iota(jnp.int32, (length, length), 0)
    column = lax.broadcasted_iota(jnp.int32, (length, length), 1)
    running = exact(jnp.where(row >= column, 1.0, 0.0).astype(f32), rate * step)
    return (step, rate, running, jnp.transpose(running))


def allowed_pairs(masks, seg_row):
    length = masks.shape[0]
    row = lax.broadcasted_iota(jnp.int32, (length, length), 0)
    column = lax.broadcasted_iota(jnp.int32, (length, length), 1)
    return (row >= column) & (masks[:, 5:6] == seg_row)


def head_within(running, running_t, head, pairs):
    gap = running[:, head : head + 1] - running_t[head : head + 1, :]
    return jnp.where(pairs, jnp.exp(jnp.minimum(gap, 0.0)), 0.0)


def lane_pairs(width):
    return [
        (slice(at, min(at + 128, width)), range(at // SSM_HEAD, min(at + 128, width) // SSM_HEAD))
        for at in range(0, width, 128)
    ]


def ssm_inner_kernel(
    x_ref, before_ref, masks_ref, seg_ref, maps_ref, maps_t_ref, cw_ref, cb_ref, sk_ref, sb_ref, dl_ref,
    rows_ref, state_ref, through_ref, carried_ref,
):
    width = x_ref.shape[2]
    masks = masks_ref[0]
    maps = maps_ref[0]
    spread = spread_matrix(width)
    before_conv = conv_input(x_ref[0], before_ref[0], masks, cw_ref, cb_ref)
    active = before_conv * jax.nn.sigmoid(before_conv)
    step, rate, running, running_t = head_steps(maps[:, 32:48], sb_ref, dl_ref)
    length = masks.shape[0]
    last = running[length - 1 : length, :]
    to_end = jnp.exp(last - running) * masks[:, 3:4]
    scaled = active * nn(step.astype(bf16), spread)
    scaled_b = scaled.astype(bf16)
    state_ref[0] = nn(
        maps_t_ref[0, :16, :].astype(bf16), (scaled * nn(to_end.astype(bf16), spread)).astype(bf16)
    )
    through = jnp.exp(last) * masks[length - 1 : length, 4:5]
    through_ref[0] = exact(jnp.broadcast_to(through, (8, PAD_HEADS)), spread.astype(f32))
    carried_ref[0] = jnp.exp(running) * masks[:, 4:5]
    pairs = allowed_pairs(masks, seg_ref[0, 0:1, :])
    inter = nt(maps[:, 16:32].astype(bf16), maps[:, :16].astype(bf16))
    for columns, heads in lane_pairs(width):
        part = scaled_b[:, columns]
        out = None
        for head in heads:
            mixed = (head_within(running, running_t, head, pairs) * inter).astype(bf16)
            mine = nn(mixed, part)
            if out is None:
                out = mine
            else:
                lane = lax.broadcasted_iota(jnp.int32, mine.shape, 1)
                out = jnp.where(lane < SSM_HEAD, out, mine)
        rows_ref[0, :, columns] = out + sk_ref[:, columns] * active[:, columns]


def ssm_outer_kernel(rows_ref, z_ref, carried_ref, maps_ref, state_ref, mask_ref, full_ref, out_ref):
    width = z_ref.shape[2]
    spread = spread_matrix(width)
    entry = nn(maps_ref[0, :, 16:32].astype(bf16), state_ref[0].astype(bf16))
    full = rows_ref[0] + nn(carried_ref[0].astype(bf16), spread) * entry
    z = z_ref[0]
    full_ref[0] = full
    out_ref[0] = (full * (z * jax.nn.sigmoid(z)) * mask_ref[...]).astype(bf16)


def ssm_direct_kernel(grad_ref, z_ref, carried_ref, maps_t_ref, mask_ref, direct_ref):
    width = z_ref.shape[2]
    z = z_ref[0]
    gated = grad_ref[0] * (z * jax.nn.sigmoid(z)) * mask_ref[...]
    weighted = gated * nn(carried_ref[0].astype(bf16), spread_matrix(width))
    direct_ref[0] = nn(maps_t_ref[0, 16:32, :].astype(bf16), weighted.astype(bf16))


def ssm_back_kernel(
    grad_ref, x_ref, z_ref, full_ref, before_ref, masks_ref, seg_ref, maps_ref, state_ref, suffix_ref,
    cw_ref, cb_ref, sk_ref, sb_ref, dl_ref, mask_ref,
    gx_ref, gz_ref, gbefore_ref, gmaps_ref, gwide_ref, ghead_ref, gscaled_ref,
):
    width = x_ref.shape[2]
    masks = masks_ref[0]
    maps = maps_ref[0]
    spread = spread_matrix(width)
    x = x_ref[0]
    before = before_ref[0]
    before_conv = conv_input(x, before, masks, cw_ref, cb_ref)
    gate = jax.nn.sigmoid(before_conv)
    active = before_conv * gate
    raw = maps[:, 32:48]
    step, rate, running, running_t = head_steps(raw, sb_ref, dl_ref)
    length = masks.shape[0]
    last = running[length - 1 : length, :]
    to_end = jnp.exp(last - running) * masks[:, 3:4]
    carried = jnp.exp(running) * masks[:, 4:5]
    through = jnp.exp(last) * masks[length - 1 : length, 4:5]
    step_wide = nn(step.astype(bf16), spread)
    scaled = active * step_wide
    scaled_b = scaled.astype(bf16)
    z = z_ref[0]
    z_gate = jax.nn.sigmoid(z)
    grad = grad_ref[0] * mask_ref[...]
    gz_ref[0] = (grad * full_ref[0] * (z_gate * (1.0 + z * (1.0 - z_gate)))).astype(bf16)
    gated = grad * (z * z_gate)
    gated_b = gated.astype(bf16)
    write_b = maps[:, :16].astype(bf16)
    read_b = maps[:, 16:32].astype(bf16)
    state = state_ref[0]
    suffix = suffix_ref[0]
    carried_gated = gated * nn(carried.astype(bf16), spread)
    ended_scaled = scaled * nn(to_end.astype(bf16), spread)
    from_state = nn(read_b, state.astype(bf16))
    from_suffix = nn(write_b, suffix.astype(bf16))
    grad_read = nt(carried_gated.astype(bf16), state.astype(bf16))
    grad_write = nt(ended_scaled.astype(bf16), suffix.astype(bf16))
    entry_term = nt((carried_gated * from_state).astype(bf16), spread)
    end_term = nt((ended_scaled * from_suffix).astype(bf16), spread)
    gthrough = nt(
        jnp.broadcast_to(jnp.sum(state * suffix, axis=0, keepdims=True), (8, width)).astype(bf16), spread
    )[0:1, :]
    pairs = allowed_pairs(masks, seg_ref[0, 0:1, :])
    inter = nt(read_b, write_b)
    grad_inter = jnp.zeros((length, length), f32)
    by_row = jnp.zeros((length, PAD_HEADS), f32)
    by_column = jnp.zeros((PAD_HEADS, length), f32)
    head_lane = lax.broadcasted_iota(jnp.int32, (length, PAD_HEADS), 1)
    head_row = lax.broadcasted_iota(jnp.int32, (PAD_HEADS, length), 0)
    for columns, heads in lane_pairs(width):
        part = scaled_b[:, columns]
        gated_part = gated_b[:, columns]
        lane = lax.broadcasted_iota(jnp.int32, gated_part.shape, 1)
        out = None
        for head in heads:
            within = head_within(running, running_t, head, pairs)
            mixed = within * inter
            in_head = lane < SSM_HEAD if head % 2 == 0 else lane >= SSM_HEAD
            mine = jnp.where(in_head, gated_part, jnp.zeros_like(gated_part))
            grad_mixed = nt(mine, part)
            grad_inter = grad_inter + grad_mixed * within
            moved = (grad_mixed * mixed).astype(bf16)
            by_row = by_row + nn(moved, jnp.where(head_lane == head, 1.0, 0.0).astype(bf16))
            by_column = by_column + nn(jnp.where(head_row == head, 1.0, 0.0).astype(bf16), moved)
            back = tn(mixed.astype(bf16), mine)
            out = back if out is None else out + back
        gscaled_ref[:, columns] = out
    grad_scaled = gscaled_ref[...] + nn(to_end.astype(bf16), spread) * from_suffix
    grad_inter_b = grad_inter.astype(bf16)
    grad_read = grad_read + nn(grad_inter_b, write_b)
    grad_write = grad_write + tn(grad_inter_b, read_b)
    grad_running = by_row - jnp.transpose(by_column) + entry_term - end_term
    at_last = jnp.sum(end_term, axis=0, keepdims=True) + gthrough * through
    row16 = lax.broadcasted_iota(jnp.int32, (length, PAD_HEADS), 0)
    grad_running = grad_running + jnp.where(row16 == length - 1, at_last, 0.0)
    row = lax.broadcasted_iota(jnp.int32, (length, length), 0)
    column = lax.broadcasted_iota(jnp.int32, (length, length), 1)
    summed = exact(jnp.where(row <= column, 1.0, 0.0).astype(f32), grad_running)
    grad_step = rate * summed + nt((grad_scaled * active).astype(bf16), spread)
    grad_raw = grad_step * jax.nn.sigmoid(raw + sb_ref[...])
    gmaps_ref[0, :, 0:16] = grad_write
    gmaps_ref[0, :, 16:32] = grad_read
    gmaps_ref[0, :, 32:48] = grad_raw
    grad_active = sk_ref[...] * gated + grad_scaled * step_wide
    grad_conv = grad_active * (gate * (1.0 + before_conv * (1.0 - gate)))
    sums = [None] * 6
    gx = cw_ref[3:4, :] * grad_conv
    sums[3] = jnp.sum(grad_conv * x, axis=0, keepdims=True)
    row8 = lax.broadcasted_iota(jnp.int32, before.shape, 0)
    row_wide = lax.broadcasted_iota(jnp.int32, x.shape, 0)
    gbefore = jnp.zeros(before.shape, f32)
    for steps in (1, 2, 3):
        k = 3 - steps
        part = grad_conv * masks[:, k : k + 1]
        sums[k] = jnp.sum(part * shifted_down(x, before, steps), axis=0, keepdims=True)
        weighted = cw_ref[k : k + 1, :] * part
        gx = gx + jnp.where(row_wide < length - steps, pltpu.roll(weighted, length - steps, 0), 0.0)
        gbefore = gbefore + jnp.where(row8 >= 8 - steps, pltpu.roll(weighted[:8], 8 - steps, 0), 0.0)
    sums[4] = jnp.sum(grad_conv, axis=0, keepdims=True)
    sums[5] = jnp.sum(gated * active, axis=0, keepdims=True)
    gx_ref[0] = gx
    gbefore_ref[0] = gbefore
    first = pl.program_id(0) == 0

    @pl.when(first)
    def _():
        gwide_ref[...] = jnp.zeros_like(gwide_ref)
        ghead_ref[...] = jnp.zeros_like(ghead_ref)

    for k in range(6):
        gwide_ref[k : k + 1, :] += sums[k]
    ghead_ref[0:1, :] += jnp.sum(grad_raw, axis=0, keepdims=True)
    ghead_ref[1:2, :] += jnp.sum(rate * step * summed, axis=0, keepdims=True)


def row_block(*shape):
    return pl.BlockSpec((1,) + shape, lambda f: (f,) + (0,) * len(shape))


def same_block(*shape):
    return pl.BlockSpec(shape, lambda f: (0,) * len(shape))


def ssm_inner(x, before, masks, seg_row, maps, maps_t, params):
    n, length, width = x.shape
    return pl.pallas_call(
        ssm_inner_kernel,
        grid=(n,),
        in_specs=[
            row_block(length, width), row_block(8, width), row_block(length, 8), row_block(8, length),
            row_block(length, 48), row_block(48, length),
            same_block(8, width), same_block(1, width), same_block(1, width),
            same_block(1, PAD_HEADS), same_block(1, PAD_HEADS),
        ],
        out_specs=[
            row_block(length, width), row_block(16, width), row_block(8, width), row_block(length, PAD_HEADS)
        ],
        out_shape=[
            jax.ShapeDtypeStruct((n, length, width), f32),
            jax.ShapeDtypeStruct((n, 16, width), f32),
            jax.ShapeDtypeStruct((n, 8, width), f32),
            jax.ShapeDtypeStruct((n, length, PAD_HEADS), f32),
        ],
    )(x, before, masks, seg_row, maps, maps_t, *params)


def ssm_outer(rows, z, carried, maps, state, mask):
    n, length, width = z.shape
    return pl.pallas_call(
        ssm_outer_kernel,
        grid=(n,),
        in_specs=[
            row_block(length, width), row_block(length, width), row_block(length, PAD_HEADS),
            row_block(length, 48), row_block(16, width), same_block(1, width),
        ],
        out_specs=[row_block(length, width), row_block(length, width)],
        out_shape=[
            jax.ShapeDtypeStruct((n, length, width), f32),
            jax.ShapeDtypeStruct((n, length, width), bf16),
        ],
    )(rows, z, carried, maps, state, mask)


def ssm_direct(grad, z, carried, maps_t, mask):
    n, length, width = z.shape
    return pl.pallas_call(
        ssm_direct_kernel,
        grid=(n,),
        in_specs=[
            row_block(length, width), row_block(length, width), row_block(length, PAD_HEADS),
            row_block(48, length), same_block(1, width),
        ],
        out_specs=row_block(16, width),
        out_shape=jax.ShapeDtypeStruct((n, 16, width), f32),
    )(grad, z, carried, maps_t, mask)


def ssm_back(grad, x, z, full, before, masks, seg_row, maps, state, suffix, params, mask):
    n, length, width = x.shape
    wide = row_block(length, width)
    return pl.pallas_call(
        ssm_back_kernel,
        grid=(n,),
        in_specs=[
            wide, wide, wide, wide, row_block(8, width), row_block(length, 8), row_block(8, length),
            row_block(length, 48), row_block(16, width), row_block(16, width),
            same_block(8, width), same_block(1, width), same_block(1, width),
            same_block(1, PAD_HEADS), same_block(1, PAD_HEADS), same_block(1, width),
        ],
        out_specs=[
            wide, wide, row_block(8, width), row_block(length, 48),
            same_block(8, width), same_block(8, PAD_HEADS),
        ],
        out_shape=[
            jax.ShapeDtypeStruct((n, length, width), f32),
            jax.ShapeDtypeStruct((n, length, width), bf16),
            jax.ShapeDtypeStruct((n, 8, width), f32),
            jax.ShapeDtypeStruct((n, length, 48), f32),
            jax.ShapeDtypeStruct((8, width), f32),
            jax.ShapeDtypeStruct((8, PAD_HEADS), f32),
        ],
        scratch_shapes=[pltpu.VMEM((length, width), f32)],
    )(grad, x, z, full, before, masks, seg_row, maps, state, suffix, *params, mask)


def entering(through, state, reverse):
    count = lax.axis_size("ctx") // 2
    place = lax.axis_index("ctx")
    z_place, second = place // 2, (place % 2 == 1) != reverse
    sent = state.astype(bf16)
    through_other = swap(through, "ctx", 1)
    state_other = swap(sent, "ctx", 1).astype(f32)

    def chain(decay, before, after):
        return decay * before + after

    pair_through = through * through_other
    pair_state = jnp.where(
        second, chain(through, state_other, state), chain(through_other, state, state_other)
    ).astype(bf16)
    entry = jnp.zeros_like(state)
    sign = -1 if reverse else 1
    for steps in range(count - 1, 0, -1):
        through_there = shift_z(pair_through, sign * steps)
        state_there = shift_z(pair_state, sign * steps).astype(f32)
        present = (z_place + steps < count) if reverse else (z_place >= steps)
        entry = jnp.where(present, chain(through_there, entry, state_there), entry)
    return jnp.where(second, chain(through_other, entry, state_other), entry)


def columns_kernel(member_ref, part0, part1, part2, part3, query_ref, keyval_ref):
    q_cols = query_ref.shape[0] // 4
    kv_cols = keyval_ref.shape[0] // 4
    for k, part in enumerate((part0, part1, part2, part3)):
        block = member_ref[0] ^ k
        turned = jnp.transpose(part[...].astype(f32))
        query_ref[pl.ds(pl.multiple_of(block * q_cols, 16), q_cols), :] = (
            turned[:q_cols] * HEAD_DIM ** (-0.5)
        ).astype(bf16)
        keyval_ref[pl.ds(pl.multiple_of(block * kv_cols, 16), kv_cols), :] = turned[q_cols:].astype(bf16)


def columns_of_tokens(parts, q_cols, kv_cols):
    rows = parts[0].shape[0]
    vmem = pl.BlockSpec(memory_space=pltpu.VMEM)
    return pl.pallas_call(
        columns_kernel,
        in_specs=[pl.BlockSpec(memory_space=pltpu.SMEM)] + [vmem] * 4,
        out_specs=[vmem, vmem],
        out_shape=[
            jax.ShapeDtypeStruct((4 * q_cols, rows), bf16),
            jax.ShapeDtypeStruct((4 * kv_cols, rows), bf16),
        ],
    )(lax.axis_index("fsdp").astype(jnp.int32).reshape(1), *parts)


def members_kernel(member_ref, query_ref, keyval_ref, out0, out1, out2, out3):
    q_cols = query_ref.shape[0] // 4
    kv_cols = keyval_ref.shape[0] // 4
    for k, out in enumerate((out0, out1, out2, out3)):
        block = member_ref[0] ^ k
        rows_q = query_ref[pl.ds(pl.multiple_of(block * q_cols, 16), q_cols), :]
        rows_kv = keyval_ref[pl.ds(pl.multiple_of(block * kv_cols, 16), kv_cols), :]
        both = jnp.concatenate([rows_q.astype(f32), rows_kv.astype(f32)], axis=0)
        out[...] = jnp.transpose(both).astype(bf16)


def columns_for_members(query_t, keyval_t):
    rows = query_t.shape[1]
    width = (query_t.shape[0] + keyval_t.shape[0]) // 4
    vmem = pl.BlockSpec(memory_space=pltpu.VMEM)
    return pl.pallas_call(
        members_kernel,
        in_specs=[pl.BlockSpec(memory_space=pltpu.SMEM), vmem, vmem],
        out_specs=[vmem] * 4,
        out_shape=[jax.ShapeDtypeStruct((rows, width), bf16)] * 4,
    )(lax.axis_index("fsdp").astype(jnp.int32).reshape(1), query_t, keyval_t)


def each_block(meta_ref, near_ref, far_ref):
    count = near_ref.shape[0]
    rows = near_ref.shape[3]
    meta = meta_ref.shape[2]
    yield (slice(0, meta), meta_ref)
    for at in range(2 * count):
        ref = (near_ref if at < count else far_ref).at[at % count]
        yield (slice(meta + at * rows, meta + (at + 1) * rows), ref)


def attend_kernel(query_ref, meta_ref, near_ref, far_ref, bias_ref, context_ref, lse_ref, key_buf, value_buf):
    group = HEADS // KV_HEADS
    for span, ref in each_block(meta_ref, near_ref, far_ref):
        key_buf[span, :] = jnp.transpose(ref[0].astype(f32)).astype(bf16)
        value_buf[:, span] = ref[1]
    keys = key_buf[...]
    values_t = value_buf[...]
    bias = bias_ref[...]
    for head in range(group):
        rows = slice(head * HEAD_DIM, (head + 1) * HEAD_DIM)
        scores = nn(keys, query_ref[rows, :]) + bias
        peak = jnp.max(scores, axis=0, keepdims=True)
        expo = jnp.exp(scores - peak)
        total = jnp.sum(expo, axis=0, keepdims=True)
        context = nn(values_t, expo.astype(bf16)) / total
        context_ref[rows, :] = context.astype(bf16)
        lse_ref[0, head : head + 1, :] = peak + jnp.log(total)


def attend_specs(query_t, meta_t, near, bias):
    count, _, _, rows = near.shape
    width = HEADS // KV_HEADS * HEAD_DIM
    wide = pl.BlockSpec((width, rows), lambda g: (g, 0))
    blocks = pl.BlockSpec((count, 2, HEAD_DIM, rows), lambda g: (0, 0, g, 0))
    meta = pl.BlockSpec((2, HEAD_DIM, meta_t.shape[2]), lambda g: (0, g, 0))
    whole = pl.BlockSpec(bias.shape, lambda g: (0, 0))
    lse = pl.BlockSpec((1, HEADS // KV_HEADS, rows), lambda g: (g, 0, 0))
    return (wide, meta, blocks, whole, lse)


def attend(query_t, meta_t, near, far, bias):
    rows = query_t.shape[1]
    length = bias.shape[0]
    wide, meta, blocks, whole, lse = attend_specs(query_t, meta_t, near, bias)
    return pl.pallas_call(
        attend_kernel,
        grid=(KV_HEADS,),
        in_specs=[wide, meta, blocks, blocks, whole],
        out_specs=[wide, lse],
        out_shape=[
            jax.ShapeDtypeStruct(query_t.shape, bf16),
            jax.ShapeDtypeStruct((KV_HEADS, HEADS // KV_HEADS, rows), f32),
        ],
        scratch_shapes=[pltpu.VMEM((length, HEAD_DIM), bf16), pltpu.VMEM((HEAD_DIM, length), bf16)],
    )(query_t, meta_t, near, far, bias)


def attend_back_kernel(
    query_ref, meta_ref, near_ref, far_ref, bias_ref, lse_ref, context_ref, grad_ref,
    gq_ref, gmeta_ref, gnear_ref, gfar_ref, key_buf, key_t_buf, value_buf, gk_buf, gv_buf,
):
    group = HEADS // KV_HEADS
    for span, ref in each_block(meta_ref, near_ref, far_ref):
        key_t_buf[:, span] = ref[0]
        key_buf[span, :] = jnp.transpose(ref[0].astype(f32)).astype(bf16)
        value_buf[span, :] = jnp.transpose(ref[1].astype(f32)).astype(bf16)
    keys = key_buf[...]
    keys_t = key_t_buf[...]
    values = value_buf[...]
    bias = bias_ref[...]
    for head in range(group):
        rows = slice(head * HEAD_DIM, (head + 1) * HEAD_DIM)
        query = query_ref[rows, :]
        grad = grad_ref[rows, :]
        delta = jnp.sum(grad.astype(f32) * context_ref[rows, :].astype(f32), axis=0, keepdims=True)
        probs = jnp.exp(nn(keys, query) + bias - lse_ref[0, head : head + 1, :])
        grad_values = nt(grad, probs.astype(bf16))
        grad_scores = (probs * (nn(values, grad) - delta)).astype(bf16)
        grad_keys = nt(query, grad_scores)
        gq_ref[rows, :] = (nn(keys_t, grad_scores) * HEAD_DIM ** (-0.5)).astype(bf16)
        if head == 0:
            gk_buf[...] = grad_keys
            gv_buf[...] = grad_values
        else:
            gk_buf[...] += grad_keys
            gv_buf[...] += grad_values
    meta = meta_ref.shape[2]
    gmeta_ref[0] = gk_buf[:, :meta]
    gmeta_ref[1] = gv_buf[:, :meta]
    for span, ref in list(each_block(meta_ref, gnear_ref, gfar_ref))[1:]:
        ref[0] = gk_buf[:, span].astype(bf16)
        ref[1] = gv_buf[:, span].astype(bf16)


def attend_back(query_t, meta_t, near, far, bias, lse, context_t, grad_t):
    length = bias.shape[0]
    wide, meta, blocks, whole, lse_spec = attend_specs(query_t, meta_t, near, bias)
    return pl.pallas_call(
        attend_back_kernel,
        grid=(KV_HEADS,),
        in_specs=[wide, meta, blocks, blocks, whole, lse_spec, wide, wide],
        out_specs=[wide, meta, blocks, blocks],
        out_shape=[
            jax.ShapeDtypeStruct(query_t.shape, bf16),
            jax.ShapeDtypeStruct(meta_t.shape, f32),
            jax.ShapeDtypeStruct(near.shape, bf16),
            jax.ShapeDtypeStruct(far.shape, bf16),
        ],
        scratch_shapes=[
            pltpu.VMEM((length, HEAD_DIM), bf16),
            pltpu.VMEM((HEAD_DIM, length), bf16),
            pltpu.VMEM((length, HEAD_DIM), bf16),
            pltpu.VMEM((HEAD_DIM, length), f32),
            pltpu.VMEM((HEAD_DIM, length), f32),
        ],
    )(query_t, meta_t, near, far, bias, lse, context_t, grad_t)


def spread_blocks(block):
    count = lax.axis_size("ctx") // 2
    near = jnp.stack([block] + [shift_z(block, steps) for steps in range(1, count)])
    return (near, swap(near, "ctx", 1))


def collect_blocks(near, far):
    count = lax.axis_size("ctx") // 2
    column = near.astype(f32) + swap(far, "ctx", 1).astype(f32)
    total = column[0]
    sent = column.astype(bf16)
    for steps in range(1, count):
        total = total + shift_z(sent[steps], -steps).astype(f32)
    return total


def block_numbers():
    count = lax.axis_size("ctx") // 2
    place = lax.axis_index("ctx")
    z_there = (place // 2 - jnp.arange(count)) % count
    return jnp.stack([2 * z_there + place % 2, 2 * z_there + 1 - place % 2])


def on_device(
    tokens,
    cotangent,
    segment_ids,
    attn_norm_gain,
    w_query,
    w_keyval,
    meta_keyvals,
    w_attn_out,
    w_mamba_in,
    w_control,
    conv_weight,
    conv_bias,
    step_bias,
    decay_log,
    skip_gain,
    w_ssm_out,
    beta_attn,
    beta_ssm,
    mlp_norm_gain,
    w_gate_up,
    w_down,
):
    inputs = tokens[0].astype(f32)
    grad_out = cotangent[0]
    seg = segment_ids[0]
    rows, features = inputs.shape
    kernel, width = conv_weight.shape
    n_ctx = lax.axis_size("ctx")
    n_z = n_ctx // 2
    n_fsdp = lax.axis_size("fsdp")
    place = lax.axis_index("ctx")
    member = lax.axis_index("fsdp")
    anchor = place * rows
    shard_rows, q_cols = w_query.shape
    kv_cols = w_keyval.shape[1]
    qkv_cols = q_cols + kv_cols
    kv_width = KV_HEADS * HEAD_DIM
    meta = meta_keyvals.shape[0]
    slot_width = SLOTS * SSM_HEAD
    padded_width = -(-slot_width // 128) * 128
    half_width = width // 2
    head_count = decay_log.shape[0]
    half_heads = head_count // 2
    state_size = (w_control.shape[1] - head_count) // 2
    first_head = half_heads * (member % 2) + (half_heads - SLOTS) * (member // 2)
    repeats = member // 2 == 1
    slot_mask = jnp.where((jnp.arange(slot_width) < SSM_HEAD) & repeats, 0.0, 1.0).astype(f32)[None]

    tail = half_width - slot_width
    mine_lo, mine_hi = w_mamba_in[:, :slot_width], w_mamba_in[:, tail:]
    crossed = swap(jnp.where(repeats, mine_lo, mine_hi), "fsdp", 2)
    kept = jnp.where(repeats, mine_hi, mine_lo)
    first_shard = jnp.concatenate(
        [jnp.pad(kept, ((0, 0), (0, padded_width - slot_width))), w_query, w_keyval], axis=1
    )
    with jax.named_scope("w_first"):
        first_own, first_oth = gather_weight(first_shard)
    with jax.named_scope("w_cross"):
        cross_own, cross_oth = gather_weight(crossed)
    attn_rows, out_cols = w_attn_out.shape
    so_rows = w_ssm_out.shape[0]
    with jax.named_scope("w_outs"):
        outs_own = lax.all_gather(
            jnp.concatenate([w_attn_out, w_ssm_out], axis=0), "ctx", axis=0, axis_index_groups=z_groups()
        )
        outs_oth = swap(outs_own, "ctx", 1)
    ao_own = outs_own[:, :attn_rows].reshape(-1, out_cols)
    ao_oth = outs_oth[:, :attn_rows].reshape(-1, out_cols)
    so_even, so_odd = own_first(outs_own[:, attn_rows:], outs_oth[:, attn_rows:])
    so_cols = jnp.stack([so_even, so_odd], axis=1).reshape(width, out_cols)
    starts = [
        SSM_HEAD * (half_heads * (m % 2) + (half_heads - SLOTS) * (m // 2)) for m in range(n_fsdp)
    ]
    so_moved = lax.all_to_all(
        jnp.stack([so_cols[s : s + slot_width] for s in starts]), "fsdp", 0, 0, tiled=True
    )
    so_full = jnp.transpose(so_moved, (1, 0, 2)).reshape(slot_width, features)

    ff_rows = w_down.shape[0]
    quarter = ff_rows // n_fsdp
    gu_cols = w_gate_up.shape[1]
    gu_view = w_gate_up.reshape(shard_rows, n_ctx // 2, n_fsdp, quarter)
    gu_moved = lax.all_to_all(jnp.transpose(gu_view, (2, 0, 1, 3)), "fsdp", 0, 0, tiled=True)

    def f_columns(part):
        view = jnp.transpose(part, (1, 0, 2, 3)).reshape(shard_rows, n_ctx // 2, 2, quarter)
        return jnp.transpose(view, (0, 2, 1, 3)).reshape(shard_rows, n_ctx * quarter)

    with jax.named_scope("w_gate"):
        gate_own, gate_oth = gather_weight(f_columns(gu_moved[:2]))
    with jax.named_scope("w_up"):
        up_own, up_oth = gather_weight(f_columns(gu_moved[2:]))
    down_moved = lax.all_to_all(
        w_down.reshape(n_fsdp, quarter, w_down.shape[1]), "fsdp", 0, 0, tiled=True
    )
    with jax.named_scope("w_down"):
        down_own, down_oth = gather_weight(
            jnp.transpose(down_moved, (1, 0, 2)).reshape(quarter, features)
        )

    def gathered(values):
        own, oth = own_first(*halves(values, 1))
        every = gather_rows(jnp.stack([own, oth]))
        return (every[:, 0], every[:, 1])

    def back_to_halves(own, oth):
        total = sum_rows(jnp.stack([own, oth], axis=1))
        return own_first(total[0], total[1])

    normed_f32, norm1_pullback = jax.vjp(rms_norm, inputs, attn_norm_gain)
    normed_own, normed_oth = gathered(normed_f32.astype(bf16))
    seg_all = gather_rows(seg)
    control_own, control_oth = own_first(*halves(w_control, 0))
    control = dot(normed_own, control_own) + dot(normed_oth, control_oth)
    first_out = dot(normed_own, first_own) + dot(normed_oth, first_oth)
    qkv = exchange(first_out[..., padded_width:].astype(bf16))
    query_t, keyval_t = columns_of_tokens(qkv, q_cols, kv_cols)
    near, far = spread_blocks(keyval_t.reshape(2, kv_width, rows))
    kept_out = first_out[..., :slot_width]
    cross_out = dot(normed_own, cross_own) + dot(normed_oth, cross_oth)
    x_rows = jnp.where(repeats, cross_out, kept_out)
    z_rows = jnp.where(repeats, kept_out, cross_out)

    numbers = block_numbers().reshape(-1)
    key_seg = jnp.take(seg.reshape(n_ctx, rows), numbers, axis=0).reshape(-1)
    key_pos = (numbers[:, None] * rows + jnp.arange(rows)[None, :]).reshape(-1)
    query_pos = anchor + jnp.arange(rows)
    query_seg = lax.dynamic_slice_in_dim(seg, anchor, rows, 0)
    visible = (key_pos[:, None] <= query_pos[None, :]) & (key_seg[:, None] == query_seg[None, :])
    bias = jnp.concatenate(
        [jnp.zeros((meta, rows), f32), jnp.where(visible, 0.0, masked_score).astype(f32)], axis=0
    )
    meta_t = jnp.transpose(meta_keyvals).reshape(2, kv_width, meta)
    context_t, lse = attend(query_t, meta_t, near, far, bias)

    start = first_head * SSM_HEAD
    pad_heads = ((0, 0), (0, PAD_HEADS - SLOTS))
    params = (
        jnp.pad(lax.dynamic_slice_in_dim(conv_weight, start, slot_width, 1), ((0, 8 - kernel), (0, 0))),
        lax.dynamic_slice_in_dim(conv_bias, start, slot_width, 0)[None],
        lax.dynamic_slice_in_dim(skip_gain, start, slot_width, 0)[None],
        jnp.pad(lax.dynamic_slice_in_dim(step_bias, first_head, SLOTS, 0)[None], pad_heads),
        jnp.pad(lax.dynamic_slice_in_dim(decay_log, first_head, SLOTS, 0)[None], pad_heads),
    )
    maps = jnp.concatenate(
        [
            control[..., : 2 * state_size],
            lax.dynamic_slice_in_dim(control, 2 * state_size + first_head, SLOTS, 2),
            jnp.zeros((n_fsdp, rows, PAD_HEADS - SLOTS), f32),
        ],
        axis=-1,
    )
    maps_t = jnp.transpose(maps, (0, 2, 1))
    padded_seg = jnp.pad(seg_all, ((0, 0), (kernel - 1, 0)), constant_values=-1)
    seg_window = lax.dynamic_slice_in_dim(padded_seg, anchor, rows + kernel - 1, 1)
    seg_rows = seg_window[:, kernel - 1 :]
    seg_before = seg_window[:, kernel - 2 : kernel - 1]
    same = [seg_window[:, k : k + rows] == seg_rows for k in range(kernel - 1)]
    same += [seg_rows == seg_rows[:, rows - 1 :], seg_rows == seg_before]
    masks = jnp.stack(
        [part.astype(f32) for part in same] + [seg_rows.astype(f32)] + [jnp.zeros(seg_rows.shape, f32)] * 2,
        axis=-1,
    )
    seg_row = jnp.broadcast_to(seg_rows.astype(f32)[:, None], (n_fsdp, 8, rows))
    before = passed_along(x_rows[:, rows - 8 :].astype(bf16), "ctx", 1).astype(f32)
    inner, state_sum, through, carried = ssm_inner(
        x_rows, before, masks, seg_row, maps, maps_t, params
    )
    through = through[:, :1]
    state_in = entering(through, state_sum, False)
    full_rows, ssm_rows = ssm_outer(inner, z_rows, carried, maps, state_in, slot_mask)

    context_halves = own_first(*halves(context_t, 0))
    every = gather_rows(jnp.transpose(jnp.stack(context_halves), (0, 2, 1)))
    contexts_own, contexts_oth = every[:, 0], every[:, 1]
    attn_cols = dot(contexts_own, ao_own) + dot(contexts_oth, ao_oth)
    attn_part = jnp.concatenate(by_member(exchange(attn_cols.astype(bf16))), axis=1).astype(f32)
    ssm_part = sum_rows(dot(ssm_rows, so_full))
    mixed, mix_pullback = jax.vjp(branch_mix, attn_part, ssm_part, beta_attn, beta_ssm)
    hidden = inputs + mixed

    normed2_f32, norm2_pullback = jax.vjp(rms_norm, hidden, mlp_norm_gain)
    n2_own, n2_oth = gathered(normed2_f32.astype(bf16))
    cot_all = gather_rows(grad_out)
    gate = dot(n2_own, gate_own) + dot(n2_oth, gate_oth)
    up = dot(n2_own, up_own) + dot(n2_oth, up_oth)
    activation_f32, gate_pullback = jax.vjp(lambda g, u: jax.nn.silu(g) * u, gate, up)
    activation = activation_f32.astype(bf16)
    f_half = activation.shape[-1] // 2
    act_own, act_oth = own_first(activation[..., :f_half], activation[..., f_half:])
    with jax.named_scope("g_down"):
        gw_down = reduce_weight(dot_rows(act_own, cot_all), dot_rows(act_oth, cot_all))
    grad_act = jnp.concatenate(
        own_first(dot_t(cot_all, down_own), dot_t(cot_all, down_oth)), axis=-1
    )
    grad_gate_f, grad_up_f = gate_pullback(grad_act)
    grad_gate = grad_gate_f.astype(bf16)
    grad_up = grad_up_f.astype(bf16)
    gn2_even, gn2_odd = back_to_halves(
        dot_t(grad_gate, gate_own) + dot_t(grad_up, up_own),
        dot_t(grad_gate, gate_oth) + dot_t(grad_up, up_oth),
    )
    grad_normed2 = joined(gn2_even, gn2_odd, 1)
    with jax.named_scope("g_gate"):
        gw_gate = reduce_weight(dot_rows(n2_own, grad_gate), dot_rows(n2_oth, grad_gate))
    with jax.named_scope("g_up"):
        gw_up = reduce_weight(dot_rows(n2_own, grad_up), dot_rows(n2_oth, grad_up))
    down_part = sum_rows(dot(act_own, down_own) + dot(act_oth, down_oth))
    output = (hidden + down_part).astype(bf16)

    gd_view = jnp.transpose(gw_down.reshape(quarter, n_fsdp, w_down.shape[1]), (1, 0, 2))
    grad_w_down = lax.all_to_all(gd_view, "fsdp", 0, 0, tiled=True).reshape(w_down.shape).astype(f32)

    def f_shards(part):
        view = jnp.transpose(part.reshape(shard_rows, 2, n_ctx // 2, quarter), (0, 2, 1, 3))
        return jnp.transpose(view.reshape(shard_rows, 2, n_ctx // 2, quarter), (1, 0, 2, 3))

    gu_back = lax.all_to_all(
        jnp.concatenate([f_shards(gw_gate), f_shards(gw_up)], axis=0), "fsdp", 0, 0, tiled=True
    )
    grad_w_gate_up = jnp.transpose(gu_back, (1, 2, 0, 3)).reshape(shard_rows, gu_cols).astype(f32)

    grad_hidden_part, grad_mlp_norm_gain = norm2_pullback(grad_normed2)
    grad_hidden = grad_out.astype(f32) + grad_hidden_part
    grad_attn_f, grad_ssm_f, grad_beta_attn, grad_beta_ssm = mix_pullback(grad_hidden)
    grad_ssm_all = gather_rows(grad_ssm_f.astype(bf16))
    grad_ssm_rows = dot_t(grad_ssm_all, so_full)
    grad_attn = grad_attn_f.astype(bf16)
    grad_attn_cols = jnp.stack(
        exchange(by_member([grad_attn[:, out_cols * b : out_cols * (b + 1)] for b in range(n_fsdp)]))
    )
    gc_even, gc_odd = back_to_halves(dot_t(grad_attn_cols, ao_own), dot_t(grad_attn_cols, ao_oth))
    grad_context_t = joined(
        jnp.transpose(gc_even.astype(bf16)), jnp.transpose(gc_odd.astype(bf16)), 0
    )
    gw_so_rows = dot_rows(ssm_rows, grad_ssm_all).astype(bf16)
    gw_so_moved = lax.all_to_all(
        jnp.transpose(gw_so_rows.reshape(slot_width, n_fsdp, out_cols), (1, 0, 2)), "fsdp", 0, 0, tiled=True
    )
    gw_so_cols = jnp.concatenate(
        [gw_so_moved[0], gw_so_moved[2][SSM_HEAD:], gw_so_moved[1], gw_so_moved[3][SSM_HEAD:]], axis=0
    ).reshape(n_z, 2, so_rows, out_cols)
    gw_so_own, gw_so_oth = own_first(gw_so_cols[:, 0], gw_so_cols[:, 1])

    def with_attn(attn_half, ssm_half):
        return jnp.concatenate([attn_half.astype(bf16).reshape(n_z, attn_rows, out_cols), ssm_half], axis=1)

    with jax.named_scope("g_outs"):
        gw_outs = reduce_weight(
            with_attn(dot_rows(contexts_own, grad_attn_cols), gw_so_own).reshape(-1, out_cols).astype(f32),
            with_attn(dot_rows(contexts_oth, grad_attn_cols), gw_so_oth).reshape(-1, out_cols),
        ).astype(f32)
    grad_w_attn_out = gw_outs[:attn_rows]
    grad_w_ssm_out = gw_outs[attn_rows:]

    direct = ssm_direct(grad_ssm_rows, z_rows, carried, maps_t, slot_mask)
    suffix = entering(through, direct, True)
    gx_f, grad_z, grad_before, grad_maps, grad_wide, grad_heads = ssm_back(
        grad_ssm_rows, x_rows, z_rows, full_rows, before, masks, seg_row, maps, state_in, suffix,
        params, slot_mask,
    )
    from_next = passed_along(grad_before.astype(bf16), "ctx", -1).astype(f32)
    grad_x = (gx_f + jnp.pad(from_next, ((0, 0), (rows - 8, 0), (0, 0)))).astype(bf16)
    grad_control = jnp.concatenate(
        [
            grad_maps[..., : 2 * state_size],
            lax.dynamic_update_slice_in_dim(
                jnp.zeros((n_fsdp, rows, head_count), f32),
                grad_maps[..., 2 * state_size : 2 * state_size + SLOTS],
                first_head,
                2,
            ),
        ],
        axis=-1,
    ).astype(bf16)
    grad_kept = jnp.where(repeats, grad_z, grad_x)
    grad_cross = jnp.where(repeats, grad_x, grad_z)
    with jax.named_scope("g_mamba"):
        mamba_cols = jnp.concatenate([grad_kept, grad_cross], axis=-1)
        gw_mamba = reduce_weight(dot_rows(normed_own, mamba_cols), dot_rows(normed_oth, mamba_cols))

    gq_t, gmeta_t, gnear, gfar = attend_back(
        query_t, meta_t, near, far, bias, lse, context_t, grad_context_t
    )
    grad_meta = jnp.transpose(gmeta_t.reshape(2 * kv_width, meta))
    grad_keyval_t = collect_blocks(gnear, gfar).astype(bf16).reshape(2 * kv_width, rows)
    gqkv_cols = jnp.stack(exchange(columns_for_members(gq_t, grad_keyval_t)))

    with jax.named_scope("g_qkv"):
        gw_qkv = reduce_weight(dot_rows(normed_own, gqkv_cols), dot_rows(normed_oth, gqkv_cols))
    gw_kept = gw_mamba[:, :slot_width]
    back_again = swap(gw_mamba[:, slot_width:], "fsdp", 2)
    grad_w_mamba_in = jnp.where(
        repeats,
        jnp.concatenate([back_again, gw_kept[:, SSM_HEAD:]], axis=1),
        jnp.concatenate([gw_kept, back_again[:, SSM_HEAD:]], axis=1),
    ).astype(f32)
    grad_w_query = gw_qkv[:, :q_cols].astype(f32)
    grad_w_keyval = gw_qkv[:, q_cols:].astype(f32)
    grad_w_control = joined(
        *own_first(dot_rows(normed_own, grad_control), dot_rows(normed_oth, grad_control)), 0
    )
    grad_first = jnp.concatenate(
        [jnp.pad(grad_kept, ((0, 0), (0, 0), (0, padded_width - slot_width))), gqkv_cols], axis=-1
    )
    grad_normed = joined(
        *back_to_halves(
            dot_t(grad_first, first_own) + dot_t(grad_cross, cross_own) + dot_t(grad_control, control_own),
            dot_t(grad_first, first_oth) + dot_t(grad_cross, cross_oth) + dot_t(grad_control, control_oth),
        ),
        1,
    )
    grad_in_part, grad_attn_norm_gain = norm1_pullback(grad_normed)
    grad_tokens = grad_hidden + grad_in_part

    def placed(part, size, at):
        zero = jnp.zeros(part.shape[:-1] + (size,), f32)
        return lax.dynamic_update_slice_in_dim(zero, part, at, part.ndim - 1)

    small = (
        grad_meta,
        grad_w_control,
        placed(grad_wide[:kernel], width, start),
        placed(grad_wide[4], width, start),
        placed(grad_heads[0, :SLOTS], head_count, first_head),
        placed(grad_heads[1, :SLOTS], head_count, first_head),
        placed(grad_wide[5], width, start),
        grad_beta_attn,
        grad_beta_ssm,
        grad_mlp_norm_gain,
    )
    flat = jnp.concatenate([part.reshape(-1) for part in small])
    block = 128 * 8 * n_ctx * n_fsdp
    padded = -(-flat.shape[0] // block) * block
    summed = all_sum(jnp.pad(flat, (0, padded - flat.shape[0])).reshape(-1, 128)).reshape(-1)
    sums = []
    offset = 0
    for part in small:
        sums.append(summed[offset : offset + part.size].reshape(part.shape))
        offset += part.size
    gain_sum = all_sum_small(grad_attn_norm_gain)
    return (
        output[None],
        grad_tokens[None],
        gain_sum,
        grad_w_query,
        grad_w_keyval,
        sums[0],
        grad_w_attn_out,
        grad_w_mamba_in,
        sums[1],
        sums[2],
        sums[3],
        sums[4],
        sums[5],
        sums[6],
        grad_w_ssm_out,
        sums[7],
        sums[8],
        sums[9],
        grad_w_gate_up,
        grad_w_down,
    )


def solution(mesh):
    split = P("ctx", "fsdp")
    tokens = P("fsdp", "ctx", None)
    whole = P()
    in_specs = (
        (tokens, tokens, P("fsdp", None), whole, split, split, whole, split, split)
        + (whole,) * 6
        + (split, whole, whole, whole, split, split)
    )
    out_specs = (
        (tokens, tokens, whole, split, split, whole, split, split)
        + (whole,) * 6
        + (split, whole, whole, whole, split, split)
    )
    return jax.shard_map(
        on_device, mesh=mesh, in_specs=in_specs, out_specs=out_specs, check_vma=False
    )
```

```python
import jax
import jax.numpy as jnp
from jax import lax
from jax.experimental import pallas as pl
from jax.experimental.pallas import tpu as pltpu
from jax.sharding import PartitionSpec as P


HEADS = 25
KV_HEADS = 5
HEAD_DIM = 64
SSM_HEAD = 64
SLOTS = 13

epsilon = 1e-05
masked_score = -1e30
highest = lax.Precision.HIGHEST
bf16 = jnp.bfloat16
f32 = jnp.float32


def swap(value, axis, mask):
    count = lax.axis_size(axis)
    return lax.ppermute(value, axis, [(source, source ^ mask) for source in range(count)])


def shift_z(value, steps):
    count = lax.axis_size("ctx")
    return lax.ppermute(value, "ctx", [(s, (s + 2 * steps) % count) for s in range(count)])


def passed_along(value, axis, steps):
    count = lax.axis_size(axis)
    first, last = (max(0, -steps), min(count, count - steps))
    return lax.ppermute(value, axis, [(source, source + steps) for source in range(first, last)])


def gather_rows(value):
    far = swap(value, "fsdp", 2)
    near = swap(value, "fsdp", 1)
    both = swap(far, "fsdp", 1)
    return jnp.stack([value, near, far, both])


def sum_rows(parts):
    received = swap(jnp.stack([parts[1], parts[3]]).astype(bf16), "fsdp", 1).astype(f32)
    mine = parts[0] + received[0]
    far = parts[2] + received[1]
    return mine + swap(far.astype(bf16), "fsdp", 2).astype(f32)


def exchange(parts):
    return [parts[0]] + [swap(parts[k], "fsdp", k) for k in (1, 2, 3)]


def by_member(parts):
    place = lax.axis_index("fsdp")

    def pick(b):
        near = jnp.where(place == 0, parts[b], parts[b ^ 1])
        return jnp.where(place < 2, near, jnp.where(place == 2, parts[b ^ 2], parts[b ^ 3]))

    return [pick(b) for b in range(4)]


def together(*values):
    return lax.optimization_barrier(values)


def z_groups():
    count = lax.axis_size("ctx")
    return [[2 * z + y for z in range(count // 2)] for y in range(2)]


def odd():
    return lax.axis_index("ctx") % 2 == 1


def own_first(even_part, odd_part):
    return (jnp.where(odd(), odd_part, even_part), jnp.where(odd(), even_part, odd_part))


def halves(values, axis):
    count = lax.axis_size("ctx")
    shape = values.shape
    length = shape[axis] // count
    view = values.reshape(shape[:axis] + (count // 2, 2, length) + shape[axis + 1 :])
    merged = shape[:axis] + (shape[axis] // 2,) + shape[axis + 1 :]
    even = lax.index_in_dim(view, 0, axis + 1, False).reshape(merged)
    odd_part = lax.index_in_dim(view, 1, axis + 1, False).reshape(merged)
    return (even, odd_part)


def joined(even, odd_part, axis):
    count = lax.axis_size("ctx")
    shape = even.shape
    split = shape[:axis] + (count // 2, shape[axis] // (count // 2)) + shape[axis + 1 :]
    both = jnp.stack([even.reshape(split), odd_part.reshape(split)], axis=axis + 1)
    return both.reshape(shape[:axis] + (2 * shape[axis],) + shape[axis + 1 :])


def gather_weight(shard):
    own = lax.all_gather(shard, "ctx", axis=0, tiled=True, axis_index_groups=z_groups())
    return (own, swap(own, "ctx", 1))


def from_other(sends):
    return [swap(send.astype(bf16), "ctx", 1) for send in sends]


def parity_sums(keeps, received):
    return jnp.concatenate(
        [(k.astype(f32) + r.astype(f32)).astype(bf16) for k, r in zip(keeps, received)], axis=1
    )


def reduce_weight(keeps, sends):
    return reduce_column(parity_sums(keeps, from_other(sends)))


def reduce_column(total):
    count = lax.axis_size("ctx") // 2
    blocks = total.reshape(count, total.shape[0] // count, total.shape[1])
    shard = lax.psum_scatter(
        blocks, "ctx", scatter_dimension=0, tiled=False, axis_index_groups=z_groups()
    )
    return together(shard)[0]


def all_sum(flat):
    steps = []
    for axis in ("fsdp", "ctx"):
        mask = 1
        while mask < lax.axis_size(axis):
            steps.append((axis, mask))
            mask *= 2
    for axis, mask in steps:
        half = flat.shape[0] // 2
        high = (lax.axis_index(axis) // mask) % 2 == 1
        low_part, high_part = flat[:half], flat[half:]
        received = swap(jnp.where(high, low_part, high_part), axis, mask)
        flat = jnp.where(high, high_part, low_part) + received
    for axis, mask in reversed(steps):
        high = (lax.axis_index(axis) // mask) % 2 == 1
        received = swap(flat, axis, mask)
        flat = jnp.concatenate(
            [jnp.where(high, received, flat), jnp.where(high, flat, received)], axis=0
        )
    return flat


def all_sum_small(value):
    for axis in ("fsdp", "ctx"):
        mask = 1
        while mask < lax.axis_size(axis):
            value = value + swap(value, axis, mask)
            mask *= 2
    return value


def rms_norm(values, gain):
    return values * lax.rsqrt(jnp.mean(values * values, axis=-1, keepdims=True) + epsilon) * gain


def branch_mix(attn_part, ssm_part, beta_attn, beta_ssm):
    return 0.5 * (rms_norm(attn_part, beta_attn) + rms_norm(ssm_part, beta_ssm))


def dot(left, right):
    return lax.dot_general(
        left, right, (((left.ndim - 1,), (0,)), ((), ())), preferred_element_type=f32
    )


def dot_t(left, right):
    return lax.dot_general(
        left, right, (((left.ndim - 1,), (1,)), ((), ())), preferred_element_type=f32
    )


def dot_rows(left, right):
    dims = tuple(range(left.ndim - 1))
    return lax.dot_general(left, right, ((dims, dims), ((), ())), preferred_element_type=f32)


def nn(left, right):
    return lax.dot_general(left, right, (((1,), (0,)), ((), ())), preferred_element_type=f32)


def nt(left, right):
    return lax.dot_general(left, right, (((1,), (1,)), ((), ())), preferred_element_type=f32)


def tn(left, right):
    return lax.dot_general(left, right, (((0,), (0,)), ((), ())), preferred_element_type=f32)


def exact(left, right):
    return lax.dot_general(
        left, right, (((1,), (0,)), ((), ())), precision=highest, preferred_element_type=f32
    )


PAD_HEADS = 16


def spread_matrix(width):
    head = lax.broadcasted_iota(jnp.int32, (PAD_HEADS, width), 0)
    column = lax.broadcasted_iota(jnp.int32, (PAD_HEADS, width), 1)
    return jnp.where(column // SSM_HEAD == head, 1.0, 0.0).astype(bf16)


def shifted_down(values, before, steps):
    moved = pltpu.roll(values, steps, 0)
    row = lax.broadcasted_iota(jnp.int32, before.shape, 0)
    top = jnp.where(row < steps, pltpu.roll(before, steps, 0), moved[:8])
    return jnp.concatenate([top, moved[8:]], axis=0)


def conv_input(x, before, masks, cw_ref, cb_ref):
    total = cb_ref[...] + cw_ref[3:4, :] * x
    for steps in (1, 2, 3):
        mask = masks[:, 3 - steps : 4 - steps]
        total = total + cw_ref[3 - steps : 4 - steps, :] * (shifted_down(x, before, steps) * mask)
    return total


def head_steps(raw, sb_ref, dl_ref):
    length = raw.shape[0]
    step = jax.nn.softplus(raw + sb_ref[...])
    rate = -jnp.exp(dl_ref[...])
    row = lax.broadcasted_iota(jnp.int32, (length, length), 0)
    column = lax.broadcasted_iota(jnp.int32, (length, length), 1)
    running = exact(jnp.where(row >= column, 1.0, 0.0).astype(f32), rate * step)
    return (step, rate, running, jnp.transpose(running))


def allowed_pairs(masks, seg_row):
    length = masks.shape[0]
    row = lax.broadcasted_iota(jnp.int32, (length, length), 0)
    column = lax.broadcasted_iota(jnp.int32, (length, length), 1)
    return (row >= column) & (masks[:, 5:6] == seg_row)


def head_within(running, running_t, head, pairs):
    gap = running[:, head : head + 1] - running_t[head : head + 1, :]
    return jnp.where(pairs, jnp.exp(jnp.minimum(gap, 0.0)), 0.0)


def lane_pairs(width):
    return [
        (slice(at, min(at + 128, width)), range(at // SSM_HEAD, min(at + 128, width) // SSM_HEAD))
        for at in range(0, width, 128)
    ]


def ssm_inner_kernel(
    x_ref, before_ref, masks_ref, seg_ref, maps_ref, maps_t_ref, cw_ref, cb_ref, sk_ref, sb_ref, dl_ref,
    rows_ref, state_ref, through_ref, carried_ref,
):
    width = x_ref.shape[2]
    masks = masks_ref[0]
    maps = maps_ref[0]
    spread = spread_matrix(width)
    before_conv = conv_input(x_ref[0], before_ref[0], masks, cw_ref, cb_ref)
    active = before_conv * jax.nn.sigmoid(before_conv)
    step, _, running, running_t = head_steps(maps[:, 32:48], sb_ref, dl_ref)
    length = masks.shape[0]
    last = running[length - 1 : length, :]
    to_end = jnp.exp(last - running) * masks[:, 3:4]
    scaled = active * nn(step.astype(bf16), spread)
    scaled_b = scaled.astype(bf16)
    state_ref[0] = nn(
        maps_t_ref[0, :16, :].astype(bf16), (scaled * nn(to_end.astype(bf16), spread)).astype(bf16)
    )
    through = jnp.exp(last) * masks[length - 1 : length, 4:5]
    through_ref[0] = exact(jnp.broadcast_to(through, (8, PAD_HEADS)), spread.astype(f32))
    carried_ref[0] = jnp.exp(running) * masks[:, 4:5]
    pairs = allowed_pairs(masks, seg_ref[0, 0:1, :])
    inter = nt(maps[:, 16:32].astype(bf16), maps[:, :16].astype(bf16))
    for columns, heads in lane_pairs(width):
        part = scaled_b[:, columns]
        out = None
        for head in heads:
            mixed = (head_within(running, running_t, head, pairs) * inter).astype(bf16)
            mine = nn(mixed, part)
            if out is None:
                out = mine
            else:
                lane = lax.broadcasted_iota(jnp.int32, mine.shape, 1)
                out = jnp.where(lane < SSM_HEAD, out, mine)
        rows_ref[0, :, columns] = out + sk_ref[:, columns] * active[:, columns]


def ssm_outer_kernel(rows_ref, z_ref, carried_ref, maps_ref, state_ref, mask_ref, full_ref, out_ref):
    width = z_ref.shape[2]
    spread = spread_matrix(width)
    entry = nn(maps_ref[0, :, 16:32].astype(bf16), state_ref[0].astype(bf16))
    full = rows_ref[0] + nn(carried_ref[0].astype(bf16), spread) * entry
    z = z_ref[0]
    full_ref[0] = full
    out_ref[0] = (full * (z * jax.nn.sigmoid(z)) * mask_ref[...]).astype(bf16)


def ssm_direct_kernel(grad_ref, z_ref, carried_ref, maps_t_ref, mask_ref, direct_ref):
    width = z_ref.shape[2]
    z = z_ref[0]
    gated = grad_ref[0] * (z * jax.nn.sigmoid(z)) * mask_ref[...]
    weighted = gated * nn(carried_ref[0].astype(bf16), spread_matrix(width))
    direct_ref[0] = nn(maps_t_ref[0, 16:32, :].astype(bf16), weighted.astype(bf16))


def ssm_back_kernel(
    grad_ref, x_ref, z_ref, full_ref, before_ref, masks_ref, seg_ref, maps_ref, state_ref, suffix_ref,
    cw_ref, cb_ref, sk_ref, sb_ref, dl_ref, mask_ref,
    gx_ref, gz_ref, gbefore_ref, gmaps_ref, gwide_ref, ghead_ref, gscaled_ref,
):
    width = x_ref.shape[2]
    masks = masks_ref[0]
    maps = maps_ref[0]
    spread = spread_matrix(width)
    x = x_ref[0]
    before = before_ref[0]
    before_conv = conv_input(x, before, masks, cw_ref, cb_ref)
    gate = jax.nn.sigmoid(before_conv)
    active = before_conv * gate
    raw = maps[:, 32:48]
    step, rate, running, running_t = head_steps(raw, sb_ref, dl_ref)
    length = masks.shape[0]
    last = running[length - 1 : length, :]
    to_end = jnp.exp(last - running) * masks[:, 3:4]
    carried = jnp.exp(running) * masks[:, 4:5]
    through = jnp.exp(last) * masks[length - 1 : length, 4:5]
    step_wide = nn(step.astype(bf16), spread)
    scaled = active * step_wide
    scaled_b = scaled.astype(bf16)
    z = z_ref[0]
    z_gate = jax.nn.sigmoid(z)
    grad = grad_ref[0] * mask_ref[...]
    gz_ref[0] = (grad * full_ref[0] * (z_gate * (1.0 + z * (1.0 - z_gate)))).astype(bf16)
    gated = grad * (z * z_gate)
    gated_b = gated.astype(bf16)
    write_b = maps[:, :16].astype(bf16)
    read_b = maps[:, 16:32].astype(bf16)
    state = state_ref[0]
    suffix = suffix_ref[0]
    carried_gated = gated * nn(carried.astype(bf16), spread)
    ended_scaled = scaled * nn(to_end.astype(bf16), spread)
    from_state = nn(read_b, state.astype(bf16))
    from_suffix = nn(write_b, suffix.astype(bf16))
    grad_read = nt(carried_gated.astype(bf16), state.astype(bf16))
    grad_write = nt(ended_scaled.astype(bf16), suffix.astype(bf16))
    entry_term = nt((carried_gated * from_state).astype(bf16), spread)
    end_term = nt((ended_scaled * from_suffix).astype(bf16), spread)
    gthrough = nt(
        jnp.broadcast_to(jnp.sum(state * suffix, axis=0, keepdims=True), (8, width)).astype(bf16), spread
    )[0:1, :]
    pairs = allowed_pairs(masks, seg_ref[0, 0:1, :])
    inter = nt(read_b, write_b)
    grad_inter = jnp.zeros((length, length), f32)
    by_row = jnp.zeros((length, PAD_HEADS), f32)
    by_column = jnp.zeros((PAD_HEADS, length), f32)
    head_lane = lax.broadcasted_iota(jnp.int32, (length, PAD_HEADS), 1)
    head_row = lax.broadcasted_iota(jnp.int32, (PAD_HEADS, length), 0)
    for columns, heads in lane_pairs(width):
        part = scaled_b[:, columns]
        gated_part = gated_b[:, columns]
        lane = lax.broadcasted_iota(jnp.int32, gated_part.shape, 1)
        out = None
        for head in heads:
            within = head_within(running, running_t, head, pairs)
            mixed = within * inter
            in_head = lane < SSM_HEAD if head % 2 == 0 else lane >= SSM_HEAD
            mine = jnp.where(in_head, gated_part, jnp.zeros_like(gated_part))
            grad_mixed = nt(mine, part)
            grad_inter = grad_inter + grad_mixed * within
            moved = (grad_mixed * mixed).astype(bf16)
            by_row = by_row + nn(moved, jnp.where(head_lane == head, 1.0, 0.0).astype(bf16))
            by_column = by_column + nn(jnp.where(head_row == head, 1.0, 0.0).astype(bf16), moved)
            back = tn(mixed.astype(bf16), mine)
            out = back if out is None else out + back
        gscaled_ref[:, columns] = out
    grad_scaled = gscaled_ref[...] + nn(to_end.astype(bf16), spread) * from_suffix
    grad_inter_b = grad_inter.astype(bf16)
    grad_read = grad_read + nn(grad_inter_b, write_b)
    grad_write = grad_write + tn(grad_inter_b, read_b)
    grad_running = by_row - jnp.transpose(by_column) + entry_term - end_term
    at_last = jnp.sum(end_term, axis=0, keepdims=True) + gthrough * through
    row16 = lax.broadcasted_iota(jnp.int32, (length, PAD_HEADS), 0)
    grad_running = grad_running + jnp.where(row16 == length - 1, at_last, 0.0)
    row = lax.broadcasted_iota(jnp.int32, (length, length), 0)
    column = lax.broadcasted_iota(jnp.int32, (length, length), 1)
    summed = exact(jnp.where(row <= column, 1.0, 0.0).astype(f32), grad_running)
    grad_step = rate * summed + nt((grad_scaled * active).astype(bf16), spread)
    grad_raw = grad_step * jax.nn.sigmoid(raw + sb_ref[...])
    gmaps_ref[0, :, 0:16] = grad_write
    gmaps_ref[0, :, 16:32] = grad_read
    gmaps_ref[0, :, 32:48] = grad_raw
    grad_active = sk_ref[...] * gated + grad_scaled * step_wide
    grad_conv = grad_active * (gate * (1.0 + before_conv * (1.0 - gate)))
    sums = [None] * 6
    gx = cw_ref[3:4, :] * grad_conv
    sums[3] = jnp.sum(grad_conv * x, axis=0, keepdims=True)
    row8 = lax.broadcasted_iota(jnp.int32, before.shape, 0)
    row_wide = lax.broadcasted_iota(jnp.int32, x.shape, 0)
    gbefore = jnp.zeros(before.shape, f32)
    for steps in (1, 2, 3):
        k = 3 - steps
        part = grad_conv * masks[:, k : k + 1]
        sums[k] = jnp.sum(part * shifted_down(x, before, steps), axis=0, keepdims=True)
        weighted = cw_ref[k : k + 1, :] * part
        gx = gx + jnp.where(row_wide < length - steps, pltpu.roll(weighted, length - steps, 0), 0.0)
        gbefore = gbefore + jnp.where(row8 >= 8 - steps, pltpu.roll(weighted[:8], 8 - steps, 0), 0.0)
    sums[4] = jnp.sum(grad_conv, axis=0, keepdims=True)
    sums[5] = jnp.sum(gated * active, axis=0, keepdims=True)
    gx_ref[0] = gx
    gbefore_ref[0] = gbefore
    first = pl.program_id(0) == 0

    @pl.when(first)
    def _():
        gwide_ref[...] = jnp.zeros_like(gwide_ref)
        ghead_ref[...] = jnp.zeros_like(ghead_ref)

    for k in range(6):
        gwide_ref[k : k + 1, :] += sums[k]
    ghead_ref[0:1, :] += jnp.sum(grad_raw, axis=0, keepdims=True)
    ghead_ref[1:2, :] += jnp.sum(rate * step * summed, axis=0, keepdims=True)


def row_block(*shape):
    return pl.BlockSpec((1,) + shape, lambda f: (f,) + (0,) * len(shape))


def same_block(*shape):
    return pl.BlockSpec(shape, lambda f: (0,) * len(shape))


def ssm_inner(x, before, masks, seg_row, maps, maps_t, params):
    n, length, width = x.shape
    return pl.pallas_call(
        ssm_inner_kernel,
        grid=(n,),
        in_specs=[
            row_block(length, width), row_block(8, width), row_block(length, 8), row_block(8, length),
            row_block(length, 48), row_block(48, length),
            same_block(8, width), same_block(1, width), same_block(1, width),
            same_block(1, PAD_HEADS), same_block(1, PAD_HEADS),
        ],
        out_specs=[
            row_block(length, width), row_block(16, width), row_block(8, width), row_block(length, PAD_HEADS)
        ],
        out_shape=[
            jax.ShapeDtypeStruct((n, length, width), f32),
            jax.ShapeDtypeStruct((n, 16, width), f32),
            jax.ShapeDtypeStruct((n, 8, width), f32),
            jax.ShapeDtypeStruct((n, length, PAD_HEADS), f32),
        ],
    )(x, before, masks, seg_row, maps, maps_t, *params)


def ssm_outer(rows, z, carried, maps, state, mask):
    n, length, width = z.shape
    return pl.pallas_call(
        ssm_outer_kernel,
        grid=(n,),
        in_specs=[
            row_block(length, width), row_block(length, width), row_block(length, PAD_HEADS),
            row_block(length, 48), row_block(16, width), same_block(1, width),
        ],
        out_specs=[row_block(length, width), row_block(length, width)],
        out_shape=[
            jax.ShapeDtypeStruct((n, length, width), f32),
            jax.ShapeDtypeStruct((n, length, width), bf16),
        ],
    )(rows, z, carried, maps, state, mask)


def ssm_direct(grad, z, carried, maps_t, mask):
    n, length, width = z.shape
    return pl.pallas_call(
        ssm_direct_kernel,
        grid=(n,),
        in_specs=[
            row_block(length, width), row_block(length, width), row_block(length, PAD_HEADS),
            row_block(48, length), same_block(1, width),
        ],
        out_specs=row_block(16, width),
        out_shape=jax.ShapeDtypeStruct((n, 16, width), f32),
    )(grad, z, carried, maps_t, mask)


def ssm_back(grad, x, z, full, before, masks, seg_row, maps, state, suffix, params, mask):
    n, length, width = x.shape
    wide = row_block(length, width)
    return pl.pallas_call(
        ssm_back_kernel,
        grid=(n,),
        in_specs=[
            wide, wide, wide, wide, row_block(8, width), row_block(length, 8), row_block(8, length),
            row_block(length, 48), row_block(16, width), row_block(16, width),
            same_block(8, width), same_block(1, width), same_block(1, width),
            same_block(1, PAD_HEADS), same_block(1, PAD_HEADS), same_block(1, width),
        ],
        out_specs=[
            wide, wide, row_block(8, width), row_block(length, 48),
            same_block(8, width), same_block(8, PAD_HEADS),
        ],
        out_shape=[
            jax.ShapeDtypeStruct((n, length, width), f32),
            jax.ShapeDtypeStruct((n, length, width), bf16),
            jax.ShapeDtypeStruct((n, 8, width), f32),
            jax.ShapeDtypeStruct((n, length, 48), f32),
            jax.ShapeDtypeStruct((8, width), f32),
            jax.ShapeDtypeStruct((8, PAD_HEADS), f32),
        ],
        scratch_shapes=[pltpu.VMEM((length, width), f32)],
    )(grad, x, z, full, before, masks, seg_row, maps, state, suffix, *params, mask)


def entering(through, state, reverse):
    count = lax.axis_size("ctx") // 2
    place = lax.axis_index("ctx")
    z_place, second = place // 2, (place % 2 == 1) != reverse
    sent = state.astype(bf16)
    state_other = swap(sent, "ctx", 1).astype(f32)
    through_other = swap(through, "ctx", 1)

    def chain(decay, before, after):
        return decay * before + after

    pair_through = through * through_other
    pair_state = jnp.where(
        second, chain(through, state_other, state), chain(through_other, state, state_other)
    ).astype(bf16)
    entry = jnp.zeros_like(state)
    sign = -1 if reverse else 1
    for steps in range(count - 1, 0, -1):
        through_there = shift_z(pair_through, sign * steps)
        state_there = shift_z(pair_state, sign * steps).astype(f32)
        present = (z_place + steps < count) if reverse else (z_place >= steps)
        entry = jnp.where(present, chain(through_there, entry, state_there), entry)
    return jnp.where(second, chain(through_other, entry, state_other), entry)


def columns_kernel(member_ref, part0, part1, part2, part3, query_ref, keyval_ref):
    q_cols = query_ref.shape[0] // 4
    kv_cols = keyval_ref.shape[0] // 4
    for k, part in enumerate((part0, part1, part2, part3)):
        block = member_ref[0] ^ k
        turned = jnp.transpose(part[...].astype(f32))
        query_ref[pl.ds(pl.multiple_of(block * q_cols, 16), q_cols), :] = (
            turned[:q_cols] * HEAD_DIM ** (-0.5)
        ).astype(bf16)
        keyval_ref[pl.ds(pl.multiple_of(block * kv_cols, 16), kv_cols), :] = turned[q_cols:].astype(bf16)


def columns_of_tokens(parts, q_cols, kv_cols):
    rows = parts[0].shape[0]
    vmem = pl.BlockSpec(memory_space=pltpu.VMEM)
    return pl.pallas_call(
        columns_kernel,
        in_specs=[pl.BlockSpec(memory_space=pltpu.SMEM)] + [vmem] * 4,
        out_specs=[vmem, vmem],
        out_shape=[
            jax.ShapeDtypeStruct((4 * q_cols, rows), bf16),
            jax.ShapeDtypeStruct((4 * kv_cols, rows), bf16),
        ],
    )(lax.axis_index("fsdp").astype(jnp.int32).reshape(1), *parts)


def members_kernel(member_ref, query_ref, keyval_ref, out0, out1, out2, out3):
    q_cols = query_ref.shape[0] // 4
    kv_cols = keyval_ref.shape[0] // 4
    for k, out in enumerate((out0, out1, out2, out3)):
        block = member_ref[0] ^ k
        rows_q = query_ref[pl.ds(pl.multiple_of(block * q_cols, 16), q_cols), :]
        rows_kv = keyval_ref[pl.ds(pl.multiple_of(block * kv_cols, 16), kv_cols), :]
        both = jnp.concatenate([rows_q.astype(f32), rows_kv.astype(f32)], axis=0)
        out[...] = jnp.transpose(both).astype(bf16)


def columns_for_members(query_t, keyval_t):
    rows = query_t.shape[1]
    width = (query_t.shape[0] + keyval_t.shape[0]) // 4
    vmem = pl.BlockSpec(memory_space=pltpu.VMEM)
    return pl.pallas_call(
        members_kernel,
        in_specs=[pl.BlockSpec(memory_space=pltpu.SMEM), vmem, vmem],
        out_specs=[vmem] * 4,
        out_shape=[jax.ShapeDtypeStruct((rows, width), bf16)] * 4,
    )(lax.axis_index("fsdp").astype(jnp.int32).reshape(1), query_t, keyval_t)


def each_block(meta_ref, near_ref, far_ref):
    count = near_ref.shape[0]
    rows = near_ref.shape[3]
    meta = meta_ref.shape[2]
    yield (slice(0, meta), meta_ref)
    for at in range(2 * count):
        ref = (near_ref if at < count else far_ref).at[at % count]
        yield (slice(meta + at * rows, meta + (at + 1) * rows), ref)


def attend_kernel(query_ref, meta_ref, near_ref, far_ref, bias_ref, context_ref, lse_ref, key_buf, value_buf):
    group = HEADS // KV_HEADS
    for span, ref in each_block(meta_ref, near_ref, far_ref):
        key_buf[span, :] = jnp.transpose(ref[0].astype(f32)).astype(bf16)
        value_buf[:, span] = ref[1]
    keys = key_buf[...]
    values_t = value_buf[...]
    bias = bias_ref[...]
    for head in range(group):
        rows = slice(head * HEAD_DIM, (head + 1) * HEAD_DIM)
        scores = nn(keys, query_ref[rows, :]) + bias
        peak = jnp.max(scores, axis=0, keepdims=True)
        expo = jnp.exp(scores - peak)
        total = jnp.sum(expo, axis=0, keepdims=True)
        context = nn(values_t, expo.astype(bf16)) / total
        context_ref[rows, :] = context.astype(bf16)
        lse_ref[0, head : head + 1, :] = peak + jnp.log(total)


def attend_specs(meta_t, near, bias):
    count, _, _, rows = near.shape
    width = HEADS // KV_HEADS * HEAD_DIM
    wide = pl.BlockSpec((width, rows), lambda g: (g, 0))
    blocks = pl.BlockSpec((count, 2, HEAD_DIM, rows), lambda g: (0, 0, g, 0))
    meta = pl.BlockSpec((2, HEAD_DIM, meta_t.shape[2]), lambda g: (0, g, 0))
    whole = pl.BlockSpec(bias.shape, lambda g: (0, 0))
    lse = pl.BlockSpec((1, HEADS // KV_HEADS, rows), lambda g: (g, 0, 0))
    return (wide, meta, blocks, whole, lse)


def attend(query_t, meta_t, near, far, bias):
    rows = query_t.shape[1]
    length = bias.shape[0]
    wide, meta, blocks, whole, lse = attend_specs(meta_t, near, bias)
    return pl.pallas_call(
        attend_kernel,
        grid=(KV_HEADS,),
        in_specs=[wide, meta, blocks, blocks, whole],
        out_specs=[wide, lse],
        out_shape=[
            jax.ShapeDtypeStruct(query_t.shape, bf16),
            jax.ShapeDtypeStruct((KV_HEADS, HEADS // KV_HEADS, rows), f32),
        ],
        scratch_shapes=[pltpu.VMEM((length, HEAD_DIM), bf16), pltpu.VMEM((HEAD_DIM, length), bf16)],
    )(query_t, meta_t, near, far, bias)


def attend_back_kernel(
    query_ref, meta_ref, near_ref, far_ref, bias_ref, lse_ref, context_ref, grad_ref,
    gq_ref, gmeta_ref, gnear_ref, gfar_ref, key_buf, key_t_buf, value_buf, gk_buf, gv_buf,
):
    group = HEADS // KV_HEADS
    for span, ref in each_block(meta_ref, near_ref, far_ref):
        key_t_buf[:, span] = ref[0]
        key_buf[span, :] = jnp.transpose(ref[0].astype(f32)).astype(bf16)
        value_buf[span, :] = jnp.transpose(ref[1].astype(f32)).astype(bf16)
    keys = key_buf[...]
    keys_t = key_t_buf[...]
    values = value_buf[...]
    bias = bias_ref[...]
    for head in range(group):
        rows = slice(head * HEAD_DIM, (head + 1) * HEAD_DIM)
        query = query_ref[rows, :]
        grad = grad_ref[rows, :]
        delta = jnp.sum(grad.astype(f32) * context_ref[rows, :].astype(f32), axis=0, keepdims=True)
        probs = jnp.exp(nn(keys, query) + bias - lse_ref[0, head : head + 1, :])
        grad_values = nt(grad, probs.astype(bf16))
        grad_scores = (probs * (nn(values, grad) - delta)).astype(bf16)
        grad_keys = nt(query, grad_scores)
        gq_ref[rows, :] = (nn(keys_t, grad_scores) * HEAD_DIM ** (-0.5)).astype(bf16)
        if head == 0:
            gk_buf[...] = grad_keys
            gv_buf[...] = grad_values
        else:
            gk_buf[...] += grad_keys
            gv_buf[...] += grad_values
    meta = meta_ref.shape[2]
    gmeta_ref[0] = gk_buf[:, :meta]
    gmeta_ref[1] = gv_buf[:, :meta]
    for span, ref in list(each_block(meta_ref, gnear_ref, gfar_ref))[1:]:
        ref[0] = gk_buf[:, span].astype(bf16)
        ref[1] = gv_buf[:, span].astype(bf16)


def attend_back(query_t, meta_t, near, far, bias, lse, context_t, grad_t):
    length = bias.shape[0]
    wide, meta, blocks, whole, lse_spec = attend_specs(meta_t, near, bias)
    return pl.pallas_call(
        attend_back_kernel,
        grid=(KV_HEADS,),
        in_specs=[wide, meta, blocks, blocks, whole, lse_spec, wide, wide],
        out_specs=[wide, meta, blocks, blocks],
        out_shape=[
            jax.ShapeDtypeStruct(query_t.shape, bf16),
            jax.ShapeDtypeStruct(meta_t.shape, f32),
            jax.ShapeDtypeStruct(near.shape, bf16),
            jax.ShapeDtypeStruct(far.shape, bf16),
        ],
        scratch_shapes=[
            pltpu.VMEM((length, HEAD_DIM), bf16),
            pltpu.VMEM((HEAD_DIM, length), bf16),
            pltpu.VMEM((length, HEAD_DIM), bf16),
            pltpu.VMEM((HEAD_DIM, length), f32),
            pltpu.VMEM((HEAD_DIM, length), f32),
        ],
    )(query_t, meta_t, near, far, bias, lse, context_t, grad_t)


def spread_blocks(block):
    count = lax.axis_size("ctx") // 2
    near = jnp.stack([block] + [shift_z(block, steps) for steps in range(1, count)])
    return (near, swap(near, "ctx", 1))


def collect_blocks(near, far):
    count = lax.axis_size("ctx") // 2
    column = near.astype(f32) + swap(far, "ctx", 1).astype(f32)
    total = column[0]
    sent = column.astype(bf16)
    for steps in range(1, count):
        total = total + shift_z(sent[steps], -steps).astype(f32)
    return total


def block_numbers():
    count = lax.axis_size("ctx") // 2
    place = lax.axis_index("ctx")
    z_there = (place // 2 - jnp.arange(count)) % count
    return jnp.stack([2 * z_there + place % 2, 2 * z_there + 1 - place % 2])


def on_device(
    tokens,
    cotangent,
    segment_ids,
    attn_norm_gain,
    w_query,
    w_keyval,
    meta_keyvals,
    w_attn_out,
    w_mamba_in,
    w_control,
    conv_weight,
    conv_bias,
    step_bias,
    decay_log,
    skip_gain,
    w_ssm_out,
    beta_attn,
    beta_ssm,
    mlp_norm_gain,
    w_gate_up,
    w_down,
):
    inputs = tokens[0].astype(f32)
    grad_out = cotangent[0]
    seg = segment_ids[0]
    rows, features = inputs.shape
    kernel, width = conv_weight.shape
    n_ctx = lax.axis_size("ctx")
    n_z = n_ctx // 2
    n_fsdp = lax.axis_size("fsdp")
    place = lax.axis_index("ctx")
    member = lax.axis_index("fsdp")
    anchor = place * rows
    shard_rows, q_cols = w_query.shape
    kv_cols = w_keyval.shape[1]
    kv_width = KV_HEADS * HEAD_DIM
    meta = meta_keyvals.shape[0]
    slot_width = SLOTS * SSM_HEAD
    padded_width = -(-slot_width // 128) * 128
    half_width = width // 2
    head_count = decay_log.shape[0]
    half_heads = head_count // 2
    state_size = (w_control.shape[1] - head_count) // 2
    first_head = half_heads * (member % 2) + (half_heads - SLOTS) * (member // 2)
    repeats = member // 2 == 1
    share = width // n_fsdp
    spare = slot_width - share
    lane = jnp.arange(slot_width)
    slot_mask = jnp.where(repeats, lane >= spare, lane < share).astype(f32)[None]

    tail = half_width - slot_width
    mine_lo, mine_hi = w_mamba_in[:, :slot_width], w_mamba_in[:, tail:]
    crossed = swap(jnp.where(repeats, mine_lo, mine_hi), "fsdp", 2)
    kept = jnp.where(repeats, mine_hi, mine_lo)
    first_shard = jnp.concatenate(
        [jnp.pad(kept, ((0, 0), (0, padded_width - slot_width))), w_query, w_keyval], axis=1
    )
    first_own, first_oth = gather_weight(first_shard)
    _, out_cols = w_attn_out.shape
    cross_shard = jnp.concatenate(
        [jnp.pad(crossed, ((0, 0), (0, padded_width - slot_width))), w_attn_out], axis=1
    )
    cross_own, cross_oth = gather_weight(cross_shard)
    ao_own, ao_oth = cross_own[:, padded_width:], cross_oth[:, padded_width:]
    so_rows = w_ssm_out.shape[0]
    so_own = lax.all_gather(w_ssm_out, "ctx", axis=0, tiled=True, axis_index_groups=z_groups())
    blocks = share // (2 * so_rows)
    quarters = [0, 2, 1, 3]
    so_quarters = so_own.reshape(n_fsdp, blocks * so_rows, out_cols)
    so_own = lax.all_to_all(jnp.stack([so_quarters[q] for q in quarters]), "fsdp", 0, 0, tiled=True)
    so_oth = swap(so_own, "ctx", 1)

    def so_side(parts):
        return jnp.transpose(parts, (1, 0, 2)).reshape(blocks, so_rows, features)

    so_mine = jnp.stack(own_first(so_side(so_own), so_side(so_oth)), axis=1).reshape(share, features)
    so_full = jnp.where(
        repeats, jnp.pad(so_mine, ((spare, 0), (0, 0))), jnp.pad(so_mine, ((0, spare), (0, 0)))
    )

    ff_rows = w_down.shape[0]
    quarter = ff_rows // n_fsdp
    padded_quarter = -(-quarter // 16) * 16
    pad_quarter = padded_quarter - quarter
    gu_cols = w_gate_up.shape[1]
    down_moved = lax.all_to_all(
        w_down.reshape(n_fsdp, quarter, w_down.shape[1]), "fsdp", 0, 0, tiled=True
    )
    gu_view = jnp.transpose(w_gate_up.reshape(shard_rows, n_ctx // 2, n_fsdp, quarter), (2, 0, 1, 3))
    gu_view, down_moved = lax.optimization_barrier((gu_view, down_moved))
    gu_moved = lax.all_to_all(gu_view, "fsdp", 0, 0, tiled=True)

    def f_columns(part):
        part = jnp.transpose(part.reshape(2, shard_rows, n_ctx // 4, 2, quarter), (1, 3, 0, 2, 4))
        view = jnp.pad(part, ((0, 0), (0, 0), (0, 0), (0, 0), (0, pad_quarter)))
        return view.reshape(shard_rows, n_ctx * padded_quarter)

    gate_own, gate_oth = gather_weight(f_columns(gu_moved[:2]))
    up_own, up_oth = gather_weight(f_columns(gu_moved[2:]))
    down_shard = jnp.pad(
        jnp.transpose(down_moved, (1, 0, 2)).reshape(quarter, features), ((0, pad_quarter), (0, 0))
    )
    down_other = swap(down_shard, "ctx", 1)
    down_own = lax.all_gather(down_shard, "ctx", axis=0, tiled=True, axis_index_groups=z_groups())
    down_oth = lax.all_gather(down_other, "ctx", axis=0, tiled=True, axis_index_groups=z_groups())

    def gathered(values):
        own, oth = own_first(*halves(values, 1))
        every = gather_rows(jnp.stack([own, oth]))
        return (every[:, 0], every[:, 1])

    def back_to_halves(own, oth):
        total = sum_rows(jnp.stack([own, oth], axis=1))
        return own_first(total[0], total[1])

    normed_f32, norm1_pullback = jax.vjp(rms_norm, inputs, attn_norm_gain)
    normed_own, normed_oth = gathered(normed_f32.astype(bf16))
    seg_all = gather_rows(seg)
    control_own, control_oth = own_first(*halves(w_control, 0))
    control = dot(normed_own, control_own) + dot(normed_oth, control_oth)
    first_out = dot(normed_own, first_own) + dot(normed_oth, first_oth)
    qkv = exchange(first_out[..., padded_width:].astype(bf16))
    query_t, keyval_t = columns_of_tokens(qkv, q_cols, kv_cols)
    near, far = spread_blocks(keyval_t.reshape(2, kv_width, rows))
    kept_out = first_out[..., :slot_width]
    cross_own, cross_oth = cross_own[:, :slot_width], cross_oth[:, :slot_width]
    cross_out = dot(normed_own, cross_own) + dot(normed_oth, cross_oth)
    x_rows = jnp.where(repeats, cross_out, kept_out)
    z_rows = jnp.where(repeats, kept_out, cross_out)

    numbers = block_numbers().reshape(-1)
    key_seg = jnp.take(seg.reshape(n_ctx, rows), numbers, axis=0).reshape(-1)
    key_pos = (numbers[:, None] * rows + jnp.arange(rows)[None, :]).reshape(-1)
    query_pos = anchor + jnp.arange(rows)
    query_seg = lax.dynamic_slice_in_dim(seg, anchor, rows, 0)
    visible = (key_pos[:, None] <= query_pos[None, :]) & (key_seg[:, None] == query_seg[None, :])
    bias = jnp.concatenate(
        [jnp.zeros((meta, rows), f32), jnp.where(visible, 0.0, masked_score).astype(f32)], axis=0
    )
    meta_t = jnp.transpose(meta_keyvals).reshape(2, kv_width, meta)
    context_t, lse = attend(query_t, meta_t, near, far, bias)

    start = first_head * SSM_HEAD
    pad_heads = ((0, 0), (0, PAD_HEADS - SLOTS))
    params = (
        jnp.pad(lax.dynamic_slice_in_dim(conv_weight, start, slot_width, 1), ((0, 8 - kernel), (0, 0))),
        lax.dynamic_slice_in_dim(conv_bias, start, slot_width, 0)[None],
        lax.dynamic_slice_in_dim(skip_gain, start, slot_width, 0)[None],
        jnp.pad(lax.dynamic_slice_in_dim(step_bias, first_head, SLOTS, 0)[None], pad_heads),
        jnp.pad(lax.dynamic_slice_in_dim(decay_log, first_head, SLOTS, 0)[None], pad_heads),
    )
    maps = jnp.concatenate(
        [
            control[..., : 2 * state_size],
            lax.dynamic_slice_in_dim(control, 2 * state_size + first_head, SLOTS, 2),
            jnp.zeros((n_fsdp, rows, PAD_HEADS - SLOTS), f32),
        ],
        axis=-1,
    )
    maps_t = jnp.transpose(maps, (0, 2, 1))
    padded_seg = jnp.pad(seg_all, ((0, 0), (kernel - 1, 0)), constant_values=-1)
    seg_window = lax.dynamic_slice_in_dim(padded_seg, anchor, rows + kernel - 1, 1)
    seg_rows = seg_window[:, kernel - 1 :]
    seg_before = seg_window[:, kernel - 2 : kernel - 1]
    same = [seg_window[:, k : k + rows] == seg_rows for k in range(kernel - 1)]
    same += [seg_rows == seg_rows[:, rows - 1 :], seg_rows == seg_before]
    masks = jnp.stack(
        [part.astype(f32) for part in same] + [seg_rows.astype(f32)] + [jnp.zeros(seg_rows.shape, f32)] * 2,
        axis=-1,
    )
    seg_row = jnp.broadcast_to(seg_rows.astype(f32)[:, None], (n_fsdp, 8, rows))
    before = passed_along(x_rows[:, rows - 8 :].astype(bf16), "ctx", 1).astype(f32)
    inner, state_sum, through, carried = ssm_inner(
        x_rows, before, masks, seg_row, maps, maps_t, params
    )
    through = through[:, :1]
    state_in = entering(through, state_sum, False)
    full_rows, ssm_rows = ssm_outer(inner, z_rows, carried, maps, state_in, slot_mask)

    context_halves = own_first(*halves(context_t, 0))
    every = gather_rows(jnp.transpose(jnp.stack(context_halves), (0, 2, 1)))
    contexts_own, contexts_oth = every[:, 0], every[:, 1]
    attn_cols = dot(contexts_own, ao_own) + dot(contexts_oth, ao_oth)
    attn_part = jnp.concatenate(by_member(exchange(attn_cols.astype(bf16))), axis=1).astype(f32)
    ssm_part = sum_rows(dot(ssm_rows, so_full))
    mixed, mix_pullback = jax.vjp(branch_mix, attn_part, ssm_part, beta_attn, beta_ssm)
    hidden = inputs + mixed

    normed2_f32, norm2_pullback = jax.vjp(rms_norm, hidden, mlp_norm_gain)
    n2_own, n2_oth = gathered(normed2_f32.astype(bf16))
    cot_all = gather_rows(grad_out)
    gate = dot(n2_own, gate_own) + dot(n2_oth, gate_oth)
    up = dot(n2_own, up_own) + dot(n2_oth, up_oth)
    activation_f32, gate_pullback = jax.vjp(lambda g, u: jax.nn.silu(g) * u, gate, up)
    activation = activation_f32.astype(bf16)
    f_half = activation.shape[-1] // 2
    act_own, act_oth = own_first(activation[..., :f_half], activation[..., f_half:])
    gw_down_send = dot_rows(act_oth, cot_all).astype(bf16)
    gw_down_keep = dot_rows(act_own, cot_all)
    gw_down_send, down_own, down_oth = together(gw_down_send, down_own, down_oth)
    gw_down = reduce_weight([gw_down_keep], [gw_down_send])
    grad_act = jnp.concatenate(
        own_first(dot_t(cot_all, down_own), dot_t(cot_all, down_oth)), axis=-1
    )
    grad_gate_f, grad_up_f = gate_pullback(grad_act)
    grad_gate = grad_gate_f.astype(bf16)
    grad_up = grad_up_f.astype(bf16)
    gn2_even, gn2_odd = back_to_halves(
        dot_t(grad_gate, gate_own) + dot_t(grad_up, up_own),
        dot_t(grad_gate, gate_oth) + dot_t(grad_up, up_oth),
    )
    grad_normed2 = joined(gn2_even, gn2_odd, 1)
    gw_gate = reduce_weight([dot_rows(n2_own, grad_gate)], [dot_rows(n2_oth, grad_gate)])
    gw_up = reduce_weight([dot_rows(n2_own, grad_up)], [dot_rows(n2_oth, grad_up)])
    down_part = sum_rows(dot(act_own, down_own) + dot(act_oth, down_oth))
    output = (hidden + down_part).astype(bf16)

    gd_view = jnp.transpose(gw_down[:quarter].reshape(quarter, n_fsdp, w_down.shape[1]), (1, 0, 2))
    gd_back = lax.all_to_all(gd_view, "fsdp", 0, 0, tiled=True)

    def f_shards(part):
        view = part.reshape(shard_rows, 2, 2, n_ctx // 4, padded_quarter)[..., :quarter]
        return jnp.transpose(view, (2, 0, 3, 1, 4)).reshape(2, shard_rows, n_ctx // 2, quarter)

    gu_back = lax.all_to_all(
        jnp.concatenate([f_shards(gw_gate), f_shards(gw_up)], axis=0), "fsdp", 0, 0, tiled=True
    )

    grad_hidden_part, grad_mlp_norm_gain = norm2_pullback(grad_normed2)
    grad_hidden = grad_out.astype(f32) + grad_hidden_part
    grad_attn_f, grad_ssm_f, grad_beta_attn, grad_beta_ssm = mix_pullback(grad_hidden)
    grad_ssm_all = gather_rows(grad_ssm_f.astype(bf16))
    grad_ssm_rows = dot_t(grad_ssm_all, so_full)
    grad_attn = grad_attn_f.astype(bf16)
    grad_attn_cols = jnp.stack(
        exchange(
            by_member([grad_attn[:, out_cols * b : out_cols * (b + 1)] for b in range(n_fsdp)])
        )
    )
    gc_even, gc_odd = back_to_halves(dot_t(grad_attn_cols, ao_own), dot_t(grad_attn_cols, ao_oth))
    grad_context_t = joined(
        jnp.transpose(gc_even.astype(bf16)), jnp.transpose(gc_odd.astype(bf16)), 0
    )
    gw_so_rows = dot_rows(ssm_rows, grad_ssm_all).astype(bf16)
    gw_so_mine = jnp.where(repeats, gw_so_rows[spare:], gw_so_rows[:share])
    gw_so_mine = gw_so_mine.reshape(blocks, 2, so_rows, features)
    gw_so_own, gw_so_oth = own_first(gw_so_mine[:, 0], gw_so_mine[:, 1])
    gw_so_received = swap(gw_so_oth, "ctx", 1)
    gw_so_sum = (gw_so_own.astype(f32) + gw_so_received.astype(f32)).astype(bf16)
    gw_so_sum = jnp.transpose(
        gw_so_sum.reshape(blocks * so_rows, n_fsdp, out_cols), (1, 0, 2)
    )
    gw_so_moved = lax.all_to_all(gw_so_sum, "fsdp", 0, 0, tiled=True)

    direct = ssm_direct(grad_ssm_rows, z_rows, carried, maps_t, slot_mask)
    suffix = entering(through, direct, True)
    gx_f, grad_z, grad_before, grad_maps, grad_wide, grad_heads = ssm_back(
        grad_ssm_rows, x_rows, z_rows, full_rows, before, masks, seg_row, maps, state_in, suffix,
        params, slot_mask,
    )
    from_next = passed_along(grad_before.astype(bf16), "ctx", -1).astype(f32)
    grad_x = (gx_f + jnp.pad(from_next, ((0, 0), (rows - 8, 0), (0, 0)))).astype(bf16)
    grad_control = jnp.concatenate(
        [
            grad_maps[..., : 2 * state_size],
            lax.dynamic_update_slice_in_dim(
                jnp.zeros((n_fsdp, rows, head_count), f32),
                grad_maps[..., 2 * state_size : 2 * state_size + SLOTS],
                first_head,
                2,
            ),
        ],
        axis=-1,
    ).astype(bf16)
    grad_kept = jnp.where(repeats, grad_z, grad_x)
    grad_cross = jnp.where(repeats, grad_x, grad_z)
    mamba_cols = jnp.concatenate([grad_kept, grad_cross], axis=-1)
    mamba_sends = [
        dot_rows(normed_oth, mamba_cols).astype(bf16),
        dot_rows(contexts_oth, grad_attn_cols).astype(bf16),
    ]
    mamba_received = from_other(mamba_sends)

    gq_t, gmeta_t, gnear, gfar = attend_back(
        query_t, meta_t, near, far, bias, lse, context_t, grad_context_t
    )
    grad_meta = jnp.transpose(gmeta_t.reshape(2 * kv_width, meta))
    grad_keyval_t = collect_blocks(gnear, gfar).astype(bf16).reshape(2 * kv_width, rows)
    gw_so_moved, grad_keyval_t = together(gw_so_moved, grad_keyval_t)
    gw_so_blocks = jnp.stack([gw_so_moved[q] for q in quarters]).reshape(n_z, so_rows, out_cols)
    grad_w_ssm_out = lax.psum_scatter(
        gw_so_blocks, "ctx", scatter_dimension=0, tiled=False, axis_index_groups=z_groups()
    ).astype(f32)
    members_columns = columns_for_members(gq_t, grad_keyval_t)
    gqkv_cols = jnp.stack(exchange(members_columns))

    qkv_received = from_other([dot_rows(normed_oth, gqkv_cols)])
    gqkv_cols, gu_back, gd_back = together(gqkv_cols, gu_back, gd_back)
    grad_w_down = gd_back.reshape(w_down.shape).astype(f32)
    grad_w_gate_up = jnp.transpose(gu_back, (1, 2, 0, 3)).reshape(shard_rows, gu_cols).astype(f32)
    grad_w_control = joined(
        *own_first(dot_rows(normed_own, grad_control), dot_rows(normed_oth, grad_control)), 0
    )
    grad_first = jnp.concatenate(
        [jnp.pad(grad_kept, ((0, 0), (0, 0), (0, padded_width - slot_width))), gqkv_cols], axis=-1
    )
    grad_normed = joined(
        *back_to_halves(
            dot_t(grad_first, first_own) + dot_t(grad_cross, cross_own) + dot_t(grad_control, control_own),
            dot_t(grad_first, first_oth) + dot_t(grad_cross, cross_oth) + dot_t(grad_control, control_oth),
        ),
        1,
    )
    grad_in_part, grad_attn_norm_gain = norm1_pullback(grad_normed)
    grad_tokens = grad_hidden + grad_in_part
    mamba_received, grad_tokens = together(mamba_received, grad_tokens)
    mamba_sums = parity_sums(
        [dot_rows(normed_own, mamba_cols), dot_rows(contexts_own, grad_attn_cols)], mamba_received
    )
    qkv_received, mamba_sums = together(qkv_received, mamba_sums)
    gw_mamba = reduce_column(mamba_sums)
    qkv_sums = parity_sums([dot_rows(normed_own, gqkv_cols)], qkv_received)
    qkv_sums, gw_mamba = together(qkv_sums, gw_mamba)
    gw_qkv = reduce_column(qkv_sums)
    grad_w_attn_out = gw_mamba[:, 2 * slot_width :].astype(f32)
    gw_kept, gw_cross = gw_mamba[:, :slot_width], gw_mamba[:, slot_width : 2 * slot_width]
    back_again = swap(gw_cross, "fsdp", 2)
    grad_w_mamba_in = jnp.where(
        repeats,
        jnp.concatenate([back_again[:, :share], gw_kept[:, spare:]], axis=1),
        jnp.concatenate([gw_kept[:, :share], back_again[:, spare:]], axis=1),
    ).astype(f32)
    grad_w_query = gw_qkv[:, :q_cols].astype(f32)
    grad_w_keyval = gw_qkv[:, q_cols:].astype(f32)

    def placed(part, size, at):
        zero = jnp.zeros(part.shape[:-1] + (size,), f32)
        return lax.dynamic_update_slice_in_dim(zero, part, at, part.ndim - 1)

    small = (
        grad_meta,
        grad_w_control,
        placed(grad_wide[:kernel], width, start),
        placed(grad_wide[4], width, start),
        placed(grad_heads[0, :SLOTS], head_count, first_head),
        placed(grad_heads[1, :SLOTS], head_count, first_head),
        placed(grad_wide[5], width, start),
        grad_beta_attn,
        grad_beta_ssm,
        grad_mlp_norm_gain,
    )
    flat = jnp.concatenate([part.reshape(-1) for part in small])
    block = 128 * 8 * n_ctx * n_fsdp
    padded = -(-flat.shape[0] // block) * block
    summed = all_sum(jnp.pad(flat, (0, padded - flat.shape[0])).reshape(-1, 128)).reshape(-1)
    sums = []
    offset = 0
    for part in small:
        sums.append(summed[offset : offset + part.size].reshape(part.shape))
        offset += part.size
    gain_sum = all_sum_small(grad_attn_norm_gain)
    return (
        output[None],
        grad_tokens[None],
        gain_sum,
        grad_w_query,
        grad_w_keyval,
        sums[0],
        grad_w_attn_out,
        grad_w_mamba_in,
        sums[1],
        sums[2],
        sums[3],
        sums[4],
        sums[5],
        sums[6],
        grad_w_ssm_out,
        sums[7],
        sums[8],
        sums[9],
        grad_w_gate_up,
        grad_w_down,
    )


def solution(mesh):
    split = P("ctx", "fsdp")
    tokens = P("fsdp", "ctx", None)
    whole = P()
    in_specs = (
        (tokens, tokens, P("fsdp", None), whole, split, split, whole, split, split)
        + (whole,) * 6
        + (split, whole, whole, whole, split, split)
    )
    out_specs = (
        (tokens, tokens, whole, split, split, whole, split, split)
        + (whole,) * 6
        + (split, whole, whole, whole, split, split)
    )

    return jax.shard_map(on_device, mesh=mesh, in_specs=in_specs, out_specs=out_specs, check_vma=False)
```
